256 devices in a mesh: grp: 8 (over z), blk: 32 (over y, x, core).
Axes of the slice: x: 4, y: 4, z: 8, core: 2. Of those that a mesh axis runs over, the one named last changes fastest.
Arguments:
- embeddings: bfloat16 [8, 2048, 1024], P('grp', 'blk'), may hold values from -72 to 72
- cluster_ids: int32 [8, 2048], P('grp', 'blk'), may hold values from 0 to 63, never falling along the last dimension, each value on 1 to 128 neighbouring positions
- block_list: int32 [8, 256, 2], P('grp', 'blk'), may hold values from 0 to 31, as said below
- block_counts: int32 [8, 32], P('grp', 'blk'), may hold values from 1 to 8, as said below
- pair_targets: float32 [8, 256, 4096], P('grp', 'blk'), may hold values from -6 to 6
- w_left: bfloat16 [1024, 512], replicated, may hold values from -0.125 to 0.125
- w_right: bfloat16 [1024, 512], replicated, may hold values from -0.125 to 0.125
- hidden_bias: float32 [512], replicated, may hold values from -3 to 3
- w_middle: bfloat16 [512, 128], replicated, may hold values from -0.25 to 0.25
- w_final: float32 [128], replicated, may hold values from -0.5 to 0.5
Outputs:
- grad_embeddings: float32 [8, 2048, 1024], P('grp', 'blk')
- grad_left: float32 [1024, 512], replicated
- grad_right: float32 [1024, 512], replicated
- grad_bias: float32 [512], replicated
- grad_middle: float32 [512, 128], replicated
- grad_final: float32 [128], replicated
The draws below stay inside these ranges and needn't reach their ends.
Inputs may be any that keep to these rules, and one draw needn't show every extreme that they name: `block_list`: entries are panels of the device's own group; the column panel lies within one of the row panel. `block_counts`: slots of a device at and beyond its count are unused; in every group one device has exactly 8.
All inputs are finite; a program needn't handle non-finite values.
Results may differ from the reference program's by a relative error of at most 0.012.
Values may be sent and summed in bfloat16 or wider, within the bound.
No kernel may reach another device: no remote copies, remote signals or barrier semaphores. Data moves between devices by JAX's collectives and lax.ppermute only.
A program may use at most 128 MiB of HBM per device.

```python
import math
import jax
import jax.numpy as jnp
import numpy as np
from jax import lax

D = 1024
H1 = 512
H2 = 128
PANEL = 64
B_DEV = 8
M_DEV = 64
PANELS = 32
MOL_G = 2048
N_GRP = 8
N_BLK = 32


def draw_embeddings(key, part):
    base = jnp.clip(jax.random.normal(jax.random.fold_in(key, 5), (N_GRP, MOL_G, D), jnp.float32), -6.0, 6.0)
    period = min(D, N_GRP * N_BLK)
    owner = jnp.arange(N_GRP, dtype=jnp.int32)[:, None] * N_BLK + jnp.arange(MOL_G, dtype=jnp.int32)[None, :] // M_DEV
    column = jnp.arange(D, dtype=jnp.int32)
    marked = column[None, None, :] % period == owner[:, :, None] % period
    return jnp.where(marked, 12.0 * base, base).astype(jnp.bfloat16)


def draw_block_list(key, part):
    key_row, key_offset = jax.random.split(jax.random.fold_in(key, 11))
    row_panel = jax.random.randint(key_row, (N_GRP, N_BLK * B_DEV), 0, PANELS)
    offset = jax.random.randint(key_offset, (N_GRP, N_BLK * B_DEV), -1, 2)
    col_panel = jnp.clip(row_panel + offset, 0, PANELS - 1)
    return jnp.stack([row_panel, col_panel], axis=-1).astype(jnp.int32)


def draw_block_counts(key, part):
    key_count, key_full = jax.random.split(jax.random.fold_in(key, 23))
    counts = jax.random.randint(key_count, (N_GRP, N_BLK), 1, B_DEV + 1)
    fullest = jax.random.randint(key_full, (N_GRP, 1), 0, N_BLK)
    positions = jnp.arange(N_BLK, dtype=jnp.int32)[None, :]
    return jnp.where(positions == fullest, B_DEV, counts).astype(jnp.int32)


def block_scale(rng, shape, cuts, least, largest):
    factor_of = 1.0
    for axis_at, blocks in cuts:
        steps = jax.random.uniform(jax.random.fold_in(jax.random.fold_in(rng, 6), axis_at), (blocks,), jnp.float32, least / len(cuts), largest / len(cuts))
        factor_of = factor_of * jnp.repeat(jnp.exp(steps), shape[axis_at] // blocks).reshape((-1,) + (1,) * (len(shape) - 1 - axis_at))
    return factor_of


def split_up(count, total, bound, lean):
    weights = [(1 << 20) // math.isqrt(rank ** lean) + 1 for rank in range(2, count + 1)]
    surplus, holding = total - bound - (count - 1), [1] * (count - 1)
    while surplus > 0:
        movable = [i for i in range(count - 1) if holding[i] < bound]
        pool, left = sum([weights[i] for i in movable]), surplus
        for i in movable:
            more = min(bound - holding[i], max(1, left * weights[i] // pool), surplus)
            holding[i] = holding[i] + more
            surplus = surplus - more
    return np.array([bound] + holding)


def uneven(own_key, count, total, limit, skew):
    if count == 2:
        one = jax.random.randint(own_key, (), max(1, total - limit), min(limit, total - 1) + 1)
        return jnp.stack([one, total - one])
    sizes = jnp.asarray(split_up(count, total, limit, skew), jnp.int32)
    couples = (count - 1) // 2
    donor, receiver = sizes[1:1 + 2 * couples:2], sizes[2:2 + 2 * couples:2]
    margin = jnp.minimum(donor - 1, limit - receiver)
    shifted = jax.random.randint(jax.random.fold_in(own_key, 1), (couples,), 0, 1 << 20) % (margin + 1)
    sizes = sizes.at[1:1 + 2 * couples:2].set(donor - shifted).at[2:2 + 2 * couples:2].set(receiver + shifted)
    return sizes[jax.random.permutation(jax.random.fold_in(own_key, 2), count)]


def scatter_about(stream_key, extent, spread, most, cuts=(), kind=jnp.bfloat16):
    gain = block_scale(stream_key, extent, cuts, -0.22, 0.18) if cuts else 1.0
    entries = jax.random.normal(stream_key, extent, jnp.float32) * spread * gain
    return jnp.minimum(jnp.maximum(entries, -most), most).astype(kind)


def setup_inputs(seed: int = 0) -> dict:
    streams_of = jax.random.split(jax.random.key(seed), 11)
    embeddings = draw_embeddings(jax.random.fold_in(streams_of[10], 71), 0)
    cluster_ids = jax.vmap(lambda own: jnp.searchsorted(jnp.cumsum(uneven(own, 2 * PANELS, MOL_G, 2 * PANEL, 1)), jnp.arange(MOL_G), side="right"))(jax.random.split(streams_of[1], N_GRP)).reshape((N_GRP, MOL_G)).astype(jnp.int32)
    block_list = draw_block_list(jax.random.fold_in(streams_of[10], 71), 0)
    block_counts = draw_block_counts(jax.random.fold_in(streams_of[10], 71), 0)
    pair_targets = scatter_about(streams_of[4], (N_GRP, N_BLK * B_DEV, PANEL * PANEL), 1.0, 6.0, ((0, 8), (1, 32)), jnp.float32)
    w_left = scatter_about(streams_of[5], (D, H1), (2 * D) ** -0.5, 0.125)
    w_right = scatter_about(streams_of[6], (D, H1), (2 * D) ** -0.5, 0.125)
    hidden_bias = scatter_about(streams_of[7], (H1,), 0.5, 3.0, (), jnp.float32)
    w_middle = scatter_about(streams_of[8], (H1, H2), H1 ** -0.5, 0.25)
    w_final = scatter_about(streams_of[9], (H2,), H2 ** -0.5, 0.5, (), jnp.float32)
    return {"embeddings": embeddings, "cluster_ids": cluster_ids, "block_list": block_list, "block_counts": block_counts, "pair_targets": pair_targets, "w_left": w_left, "w_right": w_right, "hidden_bias": hidden_bias, "w_middle": w_middle, "w_final": w_final}


def silu_slope(value):
    sigmoid_value = jax.nn.sigmoid(value)
    return sigmoid_value * (1.0 + value * (1.0 - sigmoid_value))

def pair_block(left_rows, right_rows, left_ids, right_ids, row_start, col_start, pair_target, live_factor, hidden_bias, w_middle, w_final):
    panel_rows = left_rows.shape[0]
    hidden_width = left_rows.shape[1]
    pre_hidden = left_rows.astype(jnp.float32)[:, None, :] + right_rows.astype(jnp.float32)[None, :, :] + hidden_bias
    hidden = jax.nn.silu(pre_hidden).astype(jnp.bfloat16).reshape(panel_rows * panel_rows, hidden_width)
    pre_upper = jnp.dot(hidden, w_middle, preferred_element_type=jnp.float32)
    upper_act = jax.nn.silu(pre_upper)
    predicted = lax.optimization_barrier(jnp.sum(upper_act * w_final, axis=1))
    left_pos = row_start + jnp.arange(panel_rows, dtype=jnp.int32)
    right_pos = col_start + jnp.arange(panel_rows, dtype=jnp.int32)
    same_cluster = (left_ids[:, None] == right_ids[None, :]) & (left_pos[:, None] != right_pos[None, :])
    residual = jnp.where(same_cluster.reshape(-1), predicted - pair_target, 0.0) * live_factor
    pair_slope = 16.0 * residual
    grad_final = lax.optimization_barrier(jnp.sum(upper_act * pair_slope[:, None], axis=0))
    grad_second = (pair_slope[:, None] * w_final[None, :] * silu_slope(pre_upper)).astype(jnp.bfloat16)
    grad_middle = lax.dot_general(hidden, grad_second, (((0,), (0,)), ((), ())), preferred_element_type=jnp.float32)
    grad_hidden = lax.dot_general(grad_second, w_middle, (((1,), (1,)), ((), ())), preferred_element_type=jnp.float32)
    grad_first = grad_hidden.reshape(panel_rows, panel_rows, hidden_width) * silu_slope(pre_hidden)
    return (lax.optimization_barrier(jnp.sum(grad_first, axis=1)), lax.optimization_barrier(jnp.sum(grad_first, axis=0)), lax.optimization_barrier(jnp.sum(grad_first, axis=(0, 1))), grad_middle, grad_final)

def reference(embeddings, cluster_ids, block_list, block_counts, pair_targets, w_left, w_right, hidden_bias, w_middle, w_final):
    acc_left = jnp.zeros((D, H1), jnp.float32)
    acc_right = jnp.zeros((D, H1), jnp.float32)
    acc_bias = jnp.zeros((H1,), jnp.float32)
    acc_middle = jnp.zeros((H1, H2), jnp.float32)
    acc_final = jnp.zeros((H2,), jnp.float32)
    grad_parts = []
    for group in range(N_GRP):
        group_emb = embeddings[group]
        left_all = jnp.dot(group_emb, w_left, preferred_element_type=jnp.float32).astype(jnp.bfloat16)
        right_all = jnp.dot(group_emb, w_right, preferred_element_type=jnp.float32).astype(jnp.bfloat16)
        group_ids = cluster_ids[group]
        group_blocks = block_list[group]
        group_targets = pair_targets[group]
        group_counts = block_counts[group]

        def device_step(carry, device):
            total_left, total_right, sum_bias, sum_middle, sum_final = carry
            live_count = lax.dynamic_index_in_dim(group_counts, device, 0, keepdims=False)

            def slot_step(inner, slot):
                part_left, part_right, in_bias, in_middle, in_final = inner
                slot_row = device * B_DEV + slot
                entry = lax.dynamic_index_in_dim(group_blocks, slot_row, 0, keepdims=False)
                row_start = (entry[0] * PANEL).astype(jnp.int32)
                col_start = (entry[1] * PANEL).astype(jnp.int32)
                pair_target = lax.dynamic_index_in_dim(group_targets, slot_row, 0, keepdims=False)
                live_factor = (slot < live_count).astype(jnp.float32)
                grad_rows, grad_cols, grad_bias, grad_middle, grad_final = pair_block(lax.dynamic_slice_in_dim(left_all, row_start, PANEL, 0), lax.dynamic_slice_in_dim(right_all, col_start, PANEL, 0), lax.dynamic_slice_in_dim(group_ids, row_start, PANEL, 0), lax.dynamic_slice_in_dim(group_ids, col_start, PANEL, 0), row_start, col_start, pair_target, live_factor, hidden_bias, w_middle, w_final)
                current = lax.dynamic_slice_in_dim(part_left, row_start, PANEL, 0)
                part_left = lax.dynamic_update_slice_in_dim(part_left, current + grad_rows, row_start, 0)
                current = lax.dynamic_slice_in_dim(part_right, col_start, PANEL, 0)
                part_right = lax.dynamic_update_slice_in_dim(part_right, current + grad_cols, col_start, 0)
                return ((part_left, part_right, in_bias + grad_bias, in_middle + grad_middle, in_final + grad_final), None)
            empty = jnp.zeros((MOL_G, H1), jnp.float32)
            inner, unused = lax.scan(slot_step, (empty, empty, sum_bias, sum_middle, sum_final), jnp.arange(B_DEV, dtype=jnp.int32))
            part_left, part_right, sum_bias, sum_middle, sum_final = inner
            rounded_left = lax.optimization_barrier(part_left.astype(jnp.bfloat16)).astype(jnp.float32)
            rounded_right = lax.optimization_barrier(part_right.astype(jnp.bfloat16)).astype(jnp.float32)
            return ((total_left + rounded_left, total_right + rounded_right, sum_bias, sum_middle, sum_final), None)
        start_zero = jnp.zeros((MOL_G, H1), jnp.float32)
        carry, unused = lax.scan(device_step, (start_zero, start_zero, acc_bias, acc_middle, acc_final), jnp.arange(N_BLK, dtype=jnp.int32))
        total_left, total_right, acc_bias, acc_middle, acc_final = carry
        left_grad = total_left.astype(jnp.bfloat16)
        right_grad = total_right.astype(jnp.bfloat16)
        grad_group = jnp.dot(left_grad, w_left.T, preferred_element_type=jnp.float32) + jnp.dot(right_grad, w_right.T, preferred_element_type=jnp.float32)
        grad_parts.append(grad_group)
        acc_left = acc_left + jnp.dot(group_emb.T, left_grad, preferred_element_type=jnp.float32)
        acc_right = acc_right + jnp.dot(group_emb.T, right_grad, preferred_element_type=jnp.float32)
    scale = 1.0 / jnp.sqrt(jnp.float32(N_GRP * N_BLK * B_DEV * PANEL))
    return (jnp.stack(grad_parts, axis=0), acc_left * scale, acc_right * scale, acc_bias * scale, acc_middle * scale, acc_final * scale)
```

```python
import math

import jax
import jax.numpy as jnp
from jax import lax
from jax.experimental import pallas as pl
from jax.experimental.pallas import tpu as pltpu
from jax.sharding import PartitionSpec as P

PANEL = 64
B_DEV = 8
ROWS = 8
BF = jnp.bfloat16
F32 = jnp.float32


def pair_kernel(
    flags,
    left_ref,
    right_o,
    right_m,
    right_p,
    targets_ref,
    mask_ref,
    bias_ref,
    wmt_ref,
    wf_ref,
    out_left,
    out_outer,
    out_own,
    out_partner,
    out_mid,
    out_small,
    left_s,
    right_s,
    tsum_s,
    mask_s,
    hid_s,
    slope_s,
    lacc,
    racc,
    mid_acc,
    fin_acc,
):
    hidden = left_ref.shape[1]
    tile = ROWS * PANEL
    left_s[...] = (left_ref[...].astype(F32) + bias_ref[...]) * 0.5
    for k, ref in enumerate((right_o, right_m, right_p)):
        right_s[k * PANEL : (k + 1) * PANEL, :] = ref[0:PANEL, :].astype(F32) * 0.5
    n_src = targets_ref.shape[0]
    pick = lax.rem(lax.broadcasted_iota(jnp.int32, (8, n_src), 1), 3) == lax.broadcasted_iota(
        jnp.int32, (8, n_src), 0
    )
    tsum = jnp.dot(pick.astype(BF), targets_ref[...], preferred_element_type=F32)
    for k in range(3):
        tsum_s[k, 0:1, :] = tsum[k : k + 1, :]
        mask_s[k, 0:1, :] = mask_ref[k : k + 1, :]
    lacc[...] = jnp.zeros_like(lacc)
    racc[...] = jnp.zeros_like(racc)
    mid_acc[...] = jnp.zeros_like(mid_acc)
    fin_acc[...] = jnp.zeros_like(fin_acc)

    def step(i, carry):
        @pl.when(flags[i] > 0)
        def _():
            k = i // 8
            rt = i % 8
            row0 = pl.multiple_of(rt * ROWS, ROWS)
            col0 = pl.multiple_of(k * PANEL, PANEL)
            lanes = pl.ds(pl.multiple_of(rt * tile, tile), tile)
            left8 = left_s[pl.ds(row0, ROWS), :]
            right = right_s[pl.ds(col0, PANEL), :]
            for a in range(ROWS):
                u = right + left8[a : a + 1, :]
                p = jnp.tanh(u) + 1.0
                h = u * p
                hid_s[a * PANEL : (a + 1) * PANEL, :] = h.astype(BF)
                slope_s[a * PANEL : (a + 1) * PANEL, :] = p + h * (2.0 - p)
            hid = hid_s[...]
            wmt = wmt_ref[...]
            pre = lax.dot_general(wmt, hid, (((1,), (1,)), ((), ())), preferred_element_type=F32)
            u = pre * 0.5
            p = jnp.tanh(u) + 1.0
            act = u * p
            wf = wf_ref[...]
            predicted = jnp.sum(act * wf, axis=0, keepdims=True)
            tsum = tsum_s[k, 0:1, lanes]
            count = tsum_s[k, 0:1, 8 * tile : 8 * tile + 128]
            count = jnp.concatenate([count] * (tile // 128), axis=1)
            mask = mask_s[k, 0:1, lanes]
            pair_slope = (16.0 * mask) * (count * predicted - tsum)
            grad_second = ((0.5 * pair_slope) * wf * (p + act * (2.0 - p))).astype(BF)
            fin = act * pair_slope
            fin_acc[...] += sum(fin[:, j * 128 : (j + 1) * 128] for j in range(tile // 128))
            mid_acc[...] += jnp.dot(grad_second, hid, preferred_element_type=F32)
            grad_hidden = lax.dot_general(
                grad_second, wmt, (((0,), (0,)), ((), ())), preferred_element_type=F32
            )
            cols = None
            rows = []
            for a in range(ROWS):
                g = grad_hidden[a * PANEL : (a + 1) * PANEL, :] * slope_s[a * PANEL : (a + 1) * PANEL, :]
                rows.append(jnp.sum(g, axis=0, keepdims=True))
                cols = g if cols is None else cols + g
            racc[pl.ds(col0, PANEL), :] += cols
            lacc[pl.ds(row0, ROWS), :] += jnp.concatenate(rows, axis=0)

        return carry

    lax.fori_loop(0, 24, step, 0)
    left = lacc[...] * 0.5
    out_left[...] = left.astype(BF)
    for k, ref in enumerate((out_outer, out_own, out_partner)):
        ref[...] = (racc[k * PANEL : (k + 1) * PANEL, :] * 0.5).astype(BF)
    for j in range(hidden // 128):
        block = slice(j * 128, (j + 1) * 128)
        out_mid[:, block] = mid_acc[:, block].T.astype(BF)
    out_small[...] = jnp.zeros_like(out_small)
    out_small[0:1, :] = jnp.sum(left, axis=0, keepdims=True).astype(BF)
    out_small[16:17, 0:128] = jnp.sum(fin_acc[...].T, axis=0, keepdims=True).astype(BF)


def pair_grads(flags, left, right_o, right_m, right_p, targets, mask, bias, wmt, wf):
    hidden = left.shape[1]
    upper = wmt.shape[0]
    tile = ROWS * PANEL
    vmem = pl.BlockSpec(memory_space=pltpu.VMEM)
    panel = jax.ShapeDtypeStruct((PANEL, hidden), BF)
    return pl.pallas_call(
        pair_kernel,
        out_shape=(
            panel,
            panel,
            panel,
            panel,
            jax.ShapeDtypeStruct((upper, hidden), BF),
            jax.ShapeDtypeStruct((upper, hidden), BF),
        ),
        in_specs=[pl.BlockSpec(memory_space=pltpu.SMEM)] + [vmem] * 9,
        out_specs=(vmem,) * 6,
        scratch_shapes=[
            pltpu.VMEM((PANEL, hidden), F32),
            pltpu.VMEM((3 * PANEL, hidden), F32),
            pltpu.VMEM((3, 8, targets.shape[1]), F32),
            pltpu.VMEM((3, 8, mask.shape[1]), F32),
            pltpu.VMEM((tile, hidden), BF),
            pltpu.VMEM((tile, hidden), F32),
            pltpu.VMEM((PANEL, hidden), F32),
            pltpu.VMEM((3 * PANEL, hidden), F32),
            pltpu.VMEM((upper, hidden), F32),
            pltpu.VMEM((upper, 128), F32),
        ],
        cost_estimate=pl.CostEstimate(
            flops=10 * 24 * tile * hidden * upper, bytes_accessed=2 << 20, transcendentals=24 * tile * hidden
        ),
        name="pair_grads",
    )(flags, left, right_o, right_m, right_p, targets, mask, bias, wmt, wf)


def place_kernel(pos, *refs):
    *pieces, out = refs
    shape = pieces[0].shape
    for d, ref in enumerate(pieces):
        slot = lax.rem(pos[0] - (0, 1, 3, 2)[d] + 4, 4)
        if len(out.shape) == len(shape):
            out[pl.ds(pl.multiple_of(slot * shape[0], shape[0]), shape[0]), :] = ref[...]
        else:
            out[slot] = ref[...]


def place(pos, pieces, out_shape, name):
    vmem = pl.BlockSpec(memory_space=pltpu.VMEM)
    return pl.pallas_call(
        place_kernel,
        out_shape=jax.ShapeDtypeStruct(out_shape, pieces[0].dtype),
        in_specs=[pl.BlockSpec(memory_space=pltpu.SMEM)] + [vmem] * len(pieces),
        out_specs=vmem,
        name=name,
    )(pos, *pieces)


def finish_kernel(scale, core, mine_ref, theirs_ref, left_ref, right_ref, mid_ref, bias_ref, fin_ref):
    depth = left_ref.shape[0]

    def write(first, second):
        for j in range(4):
            block = slice(j * 128, (j + 1) * 128)
            left_ref[:, block] = first[j, 0:depth, :].astype(F32) * scale
            right_ref[:, block] = second[j, 0:depth, :].astype(F32) * scale
            mid_ref[block, :] = first[j, depth : depth + 128, :].astype(F32) * scale
            bias_ref[:, block] = second[j, depth : depth + 1, :].astype(F32) * scale
        fin_ref[...] = second[0, depth + 16 : depth + 17, :].astype(F32) * scale

    @pl.when(core[0] == 0)
    def _():
        write(mine_ref, theirs_ref)

    @pl.when(core[0] != 0)
    def _():
        write(theirs_ref, mine_ref)


def local(
    embeddings,
    cluster_ids,
    block_list,
    block_counts,
    pair_targets,
    w_left,
    w_right,
    hidden_bias,
    w_middle,
    w_final,
):
    emb = embeddings[0]
    depth = emb.shape[1]
    hidden = w_left.shape[1]
    upper = w_middle.shape[1]
    panels = lax.axis_size("blk")
    groups = lax.axis_size("grp")
    me = lax.axis_index("blk")
    core, x, y = me % 2, (me // 2) % 4, me // 8

    def blk(value, partner):
        return lax.ppermute(value, "blk", [(i, partner(i)) for i in range(panels)])

    def on_core(value):
        return blk(value, lambda i: i ^ 1)

    def on_outer(value):
        return blk(value, lambda i: (i - 1 if i % 2 == 0 else i + 1) % panels)

    def on_x(value, d):
        return blk(value, lambda i: i // 8 * 8 + (i // 2 % 4 + d) % 4 * 2 + i % 2)

    def on_y(value, d):
        return blk(value, lambda i: (i // 8 + d) % 4 * 8 + i % 8)

    def on_z(value, d):
        return lax.ppermute(value, "grp", [(i, (i + d) % groups) for i in range(groups)])

    entry = block_list[0]
    row, col = entry[:, 0], entry[:, 1]
    step = jnp.where(row % 2 == 0, col - row, row - col)
    slot_of = jnp.where(jnp.arange(B_DEV) < block_counts[0, 0], row * 3 + step + 1, -1)
    place_at = (jnp.arange(3 * panels, dtype=jnp.int32)[:, None] == slot_of[None, :]).astype(BF)
    values = jnp.concatenate(
        [pair_targets[0].astype(BF), jnp.ones((B_DEV, 128), BF)], axis=1
    )
    sums = jnp.dot(place_at, values, preferred_element_type=F32).astype(BF)
    targets = lax.all_to_all(sums, "blk", 0, 0, tiled=True)

    left = jnp.dot(emb, w_left, preferred_element_type=F32).astype(BF)
    right = jnp.dot(emb, w_right, preferred_element_type=F32).astype(BF)
    ids = cluster_ids[0].astype(BF)
    ids_row = jnp.pad(ids[None, :], ((0, 15), (0, hidden - PANEL)))
    right_own = jnp.concatenate([right, ids_row], axis=0)
    right_outer = on_outer(right_own)
    right_partner = on_core(right_own)
    col_ids = jnp.stack([right_outer[PANEL, :PANEL], ids, right_partner[PANEL, :PANEL]])
    same = ids[None, :, None] == col_ids[:, None, :]
    at = jnp.arange(PANEL)
    own = (jnp.arange(3) == 1)[:, None, None] & (at[:, None] == at[None, :])[None]
    mask = (same & ~own).reshape(3, PANEL * PANEL).astype(F32)
    flags = jnp.max(mask.reshape(24, ROWS * PANEL), axis=1).astype(jnp.int32)

    lg, r_outer, r_own, r_partner, mid, small = pair_grads(
        flags,
        left,
        right_outer,
        right_own,
        right_partner,
        targets,
        mask,
        hidden_bias[None, :],
        w_middle.T,
        w_final[:, None],
    )

    emb_pair = jnp.concatenate([emb, on_core(emb)], axis=0)
    emb_all = jnp.concatenate([emb_pair] + [on_x(emb_pair, d) for d in (1, 3, 2)], axis=0)

    first = core == 0
    r_own = (r_own.astype(F32) + on_outer(r_outer).astype(F32)).astype(BF)
    sent = jnp.concatenate(
        [jnp.where(first, r_own, lg), r_partner, jnp.where(first, small, mid)], axis=0
    )
    got = on_core(sent)
    rg = (r_own.astype(F32) + got[PANEL : 2 * PANEL].astype(F32)).astype(BF)
    pair_right = (got[:PANEL].astype(F32) + r_partner.astype(F32)).astype(BF)
    extra = jnp.where(first, mid, small).astype(F32) + got[2 * PANEL :].astype(F32)
    both = jnp.concatenate(
        [jnp.where(first, lg, rg), jnp.where(first, got[:PANEL], pair_right), extra.astype(BF)], axis=0
    )
    grad_local = jnp.dot(lg, w_left.T, preferred_element_type=F32) + jnp.dot(
        rg, w_right.T, preferred_element_type=F32
    )

    def column(d):
        return lax.dynamic_slice_in_dim(both, (x + d) % 4 * 128, 128, 1)

    parts = [column(0)] + [on_x(column(d), d) for d in (1, 3, 2)]
    grads = jnp.concatenate([p[: 2 * PANEL] for p in parts], axis=0)
    weight = lax.dot_general(emb_all, grads, (((0,), (0,)), ((), ())), preferred_element_type=F32)
    extra = sum(p[2 * PANEL :].astype(F32) for p in parts)
    total = jnp.concatenate([weight, extra], axis=0).astype(BF)
    piece = total.shape[0] // 4

    def rows(d):
        return lax.dynamic_slice_in_dim(total, (y + d) % 4 * piece, piece, 0)

    parts = [rows(0)] + [on_y(rows(d), d) for d in (1, 3, 2)]
    total = sum(p.astype(F32) for p in parts).astype(BF)
    total = (
        total.astype(F32)
        + lax.ppermute(total, "grp", [(i, i ^ 1) for i in range(groups)]).astype(F32)
    ).astype(BF)
    total = sum(p.astype(F32) for p in [total] + [on_z(total, d) for d in (2, 6, 4)]).astype(BF)

    total = place(
        y[None], [total] + [on_y(total, d) for d in (1, 3, 2)], (4 * piece, 128), "place_rows"
    )
    mine = place(
        x[None], [total] + [on_x(total, d) for d in (1, 3, 2)], (4, 4 * piece, 128), "place_columns"
    )
    theirs = on_core(mine)
    devices = panels * groups
    scale = 1.0 / math.sqrt(devices * B_DEV * PANEL)
    vmem = pl.BlockSpec(memory_space=pltpu.VMEM)
    grad_left, grad_right, grad_middle, grad_bias, grad_final = pl.pallas_call(
        lambda *refs: finish_kernel(scale, *refs),
        out_shape=(
            jax.ShapeDtypeStruct((depth, hidden), F32),
            jax.ShapeDtypeStruct((depth, hidden), F32),
            jax.ShapeDtypeStruct((hidden, upper), F32),
            jax.ShapeDtypeStruct((1, hidden), F32),
            jax.ShapeDtypeStruct((1, upper), F32),
        ),
        in_specs=[pl.BlockSpec(memory_space=pltpu.SMEM), vmem, vmem],
        out_specs=(vmem,) * 5,
        name="finish",
    )(core[None], mine, theirs)
    return (grad_local[None], grad_left, grad_right, grad_bias[0], grad_middle, grad_final[0])


def solution(mesh):
    return jax.shard_map(
        local,
        mesh=mesh,
        in_specs=(
            P("grp", "blk", None),
            P("grp", "blk"),
            P("grp", "blk", None),
            P("grp", "blk"),
            P("grp", "blk", None),
            P(),
            P(),
            P(),
            P(),
            P(),
        ),
        out_specs=(P("grp", "blk", None), P(), P(), P(), P(), P()),
        check_vma=False,
    )
```

```python
import math

import jax
import jax.numpy as jnp
from jax import lax
from jax.experimental import pallas as pl
from jax.experimental.pallas import tpu as pltpu
from jax.sharding import PartitionSpec as P

PANEL = 64
B_DEV = 8
ROWS = 8
CHUNK = 256
BF = jnp.bfloat16
F32 = jnp.float32


def forward(tile_at, left_s, right_s, hid_s, slope_s, rows=range(ROWS)):
    k = tile_at // 8
    left8 = left_s[pl.ds(pl.multiple_of(tile_at % 8 * ROWS, ROWS), ROWS), :]
    right = right_s[pl.ds(pl.multiple_of(k * PANEL, PANEL), PANEL), :]
    for a in rows:
        part = slice(a * PANEL, (a + 1) * PANEL)
        u = right.astype(BF) + jnp.broadcast_to(left8[a : a + 1, :], right.shape).astype(BF)
        p = jnp.tanh(u) + BF(1.0)
        h = u * p
        hid_s[part, :] = h
        slope_s[part, :] = p + h * (BF(2.0) - p)


def backward(
    tile_at, hid_s, slope_s, tsum_s, mask_s, half_s, wmt_ref, wf_ref, lacc, racc, mid_acc, fin_acc
):
    col0 = pl.multiple_of(tile_at // 8 * PANEL, PANEL)
    row0 = pl.multiple_of(tile_at % 8 * ROWS, ROWS)
    wf = wf_ref[...]
    count = tsum_s[tile_at // 8 * 8 + 24, 0:1, 0:CHUNK]
    parts = [slice(c * CHUNK, (c + 1) * CHUNK) for c in range(ROWS * PANEL // CHUNK)]
    pre = [
        jnp.dot(hid_s[part, :], half_s[...], preferred_element_type=F32).T
        for part in parts
    ]
    terms, hiddens, fins = [], [], []
    for part, u in zip(parts, pre):
        p = jnp.tanh(u) + 1.0
        act = u * p
        predicted = jnp.sum(act * wf, axis=0, keepdims=True)
        pair_slope = (16.0 * mask_s[tile_at, 0:1, part]) * (count * predicted - tsum_s[tile_at, 0:1, part])
        grad_second = ((0.5 * pair_slope) * wf * (p + act * (2.0 - p))).astype(BF)
        fin = act * pair_slope
        fins.append(sum(fin[:, j * 128 : (j + 1) * 128] for j in range(CHUNK // 128)))
        hiddens.append(
            lax.dot_general(grad_second, wmt_ref[...], (((0,), (0,)), ((), ())), preferred_element_type=F32)
        )
        terms.append(jnp.dot(grad_second, hid_s[part, :], preferred_element_type=F32))
    fin_acc[...] += sum(fins)
    cols, rows = None, []
    for part, grad_hidden in zip(parts, hiddens):
        for a in range(CHUNK // PANEL):
            at = slice(part.start + a * PANEL, part.start + (a + 1) * PANEL)
            g = grad_hidden[a * PANEL : (a + 1) * PANEL, :] * slope_s[at, :].astype(F32)
            rows.append(jnp.sum(g, axis=0, keepdims=True))
            cols = g if cols is None else cols + g
    mid_acc[...] += sum(terms)
    racc[pl.ds(col0, PANEL), :] += cols
    lacc[pl.ds(row0, ROWS), :] += jnp.concatenate(rows, axis=0)


def pair_kernel(
    core,
    ids_s,
    ids_ref,
    left_ref,
    right_o,
    right_m,
    right_p,
    targets_ref,
    bias_ref,
    wmt_ref,
    wf_ref,
    out_left,
    out_outer,
    out_own,
    out_keep,
    out_sent,
    todo,
    left_s,
    right_s,
    tsum_s,
    mask_s,
    half_s,
    hid_s,
    slope_s,
    lacc,
    racc,
    mid_acc,
    fin_acc,
):
    hidden = left_ref.shape[1]
    tile = ROWS * PANEL
    iota = lambda shape, axis: lax.broadcasted_iota(jnp.int32, shape, axis)
    def scan(i, n):
        k, rt = i // 8, i % 8
        meets = (ids_s[1, rt * ROWS] <= ids_s[k, PANEL - 1]) & (ids_s[k, 0] <= ids_s[1, rt * ROWS + ROWS - 1])
        todo[n] = i
        return n + meets.astype(jnp.int32)

    n_todo = lax.fori_loop(0, 24, scan, 0)
    for extra in range(3):
        todo[n_todo + extra] = 24
    left_s[...] = (left_ref[...].astype(F32) + bias_ref[...]) * 0.5
    for k, ref in enumerate((right_o, right_m, right_p)):
        right_s[k * PANEL : (k + 1) * PANEL, :] = ref[0:PANEL, :].astype(F32) * 0.5
    right_s[3 * PANEL :, :] = jnp.zeros((PANEL, hidden), F32)
    half_s[...] = (wmt_ref[...].astype(F32) * 0.5).T.astype(BF)
    n_src = targets_ref.shape[0]
    tsum = jnp.dot(
        (iota((24, n_src), 1) % 24 == iota((24, n_src), 0)).astype(BF), targets_ref[...], preferred_element_type=F32
    )
    ids = ids_ref[...]
    spread = (iota((PANEL, tile), 0) % ROWS == iota((PANEL, tile), 1) // PANEL).astype(BF)
    repeat = (iota((PANEL, tile), 0) == iota((PANEL, tile), 1) % PANEL).astype(BF)
    row_ids = jnp.where(iota((8, PANEL), 1) // ROWS == iota((8, PANEL), 0), ids[1:2, :], 0.0)
    row_ids = jnp.dot(row_ids.astype(BF), spread, preferred_element_type=F32)
    col_ids = jnp.dot(ids.astype(BF), repeat, preferred_element_type=F32)
    lane = iota((8, tile), 1)
    itself = iota((8, tile), 0) * ROWS + lane // PANEL == lane % PANEL
    for k in range(3):
        same = row_ids == col_ids[k : k + 1, :]
        mask = jnp.where(same & ~itself if k == 1 else same, 1.0, 0.0)
        count = jnp.max(
            jnp.where(iota((8, tile), 1) == k * (PANEL + 1), tsum[8:16, :], 0.0)[0:1], axis=1, keepdims=True
        )
        tsum_s[24 + 8 * k, 0:1, :] = jnp.broadcast_to(count, (1, tile))
        for rt in range(8):
            mask_s[k * 8 + rt, 0:1, :] = mask[rt : rt + 1, :]
            tsum_s[k * 8 + rt, 0:1, :] = tsum[k * 8 + rt : k * 8 + rt + 1, :]
    mask_s[24, 0:1, :] = jnp.zeros((1, tile), F32)
    tsum_s[48, 0:1, :] = jnp.zeros((1, tile), F32)
    lacc[...] = jnp.zeros_like(lacc)
    racc[...] = jnp.zeros_like(racc)
    mid_acc[...] = jnp.zeros_like(mid_acc)
    fin_acc[...] = jnp.zeros_like(fin_acc)
    rest = (tsum_s, mask_s, half_s, wmt_ref, wf_ref, lacc, racc, mid_acc, fin_acc)
    def step(i, carry):
        forward(todo[i], left_s, right_s, hid_s, slope_s)
        backward(todo[i], hid_s, slope_s, *rest)
        return carry

    lax.fori_loop(0, n_todo, step, 0)
    left = lacc[...] * 0.5
    out_left[...] = left.astype(BF)
    outer, own, partner = [
        (racc[k * PANEL : (k + 1) * PANEL, :] * 0.5).astype(BF) for k in range(3)
    ]
    out_outer[...] = outer
    out_own[...] = own
    out_sent[PANEL : 2 * PANEL, :] = partner

    def middle(ref, start):
        for j in range(hidden // 128):
            block = slice(j * 128, (j + 1) * 128)
            ref[start : start + 128, block] = mid_acc[:, block].T.astype(BF)

    def small(ref, start):
        ref[start : start + 128, :] = jnp.zeros((128, hidden), BF)
        ref[start : start + 1, :] = jnp.sum(left, axis=0, keepdims=True).astype(BF)
        ref[start + 16 : start + 17, 0:128] = jnp.sum(fin_acc[...].T, axis=0, keepdims=True).astype(BF)

    @pl.when(core[0] == 0)
    def _():
        out_sent[0:PANEL, :] = own
        small(out_sent, 2 * PANEL)
        middle(out_keep, 0)

    @pl.when(core[0] != 0)
    def _():
        out_sent[0:PANEL, :] = left.astype(BF)
        middle(out_sent, 2 * PANEL)
        small(out_keep, 0)


def pair_grads(core, ids_s, ids, left, right_o, right_m, right_p, targets, bias, wmt, wf):
    hidden = left.shape[1]
    upper = wmt.shape[0]
    tile = ROWS * PANEL
    vmem = pl.BlockSpec(memory_space=pltpu.VMEM)
    panel = jax.ShapeDtypeStruct((PANEL, hidden), BF)
    return pl.pallas_call(
        pair_kernel,
        out_shape=(
            panel,
            panel,
            panel,
            jax.ShapeDtypeStruct((upper, hidden), BF),
            jax.ShapeDtypeStruct((2 * PANEL + upper, hidden), BF),
        ),
        in_specs=[pl.BlockSpec(memory_space=pltpu.SMEM)] * 2 + [vmem] * 9,
        out_specs=(vmem,) * 5,
        scratch_shapes=[
            pltpu.SMEM((32,), jnp.int32),
            pltpu.VMEM((PANEL, hidden), F32),
            pltpu.VMEM((4 * PANEL, hidden), F32),
            pltpu.VMEM((49, 8, tile), F32),
            pltpu.VMEM((25, 8, tile), F32),
            pltpu.VMEM((hidden, upper), BF),
            pltpu.VMEM((tile, hidden), BF),
            pltpu.VMEM((tile, hidden), BF),
            pltpu.VMEM((PANEL, hidden), F32),
            pltpu.VMEM((4 * PANEL, hidden), F32),
            pltpu.VMEM((upper, hidden), F32),
            pltpu.VMEM((upper, 128), F32),
        ],
        compiler_params=pltpu.CompilerParams(vmem_limit_bytes=24 << 20),
        cost_estimate=pl.CostEstimate(
            flops=10 * 24 * tile * hidden * upper, bytes_accessed=2 << 20, transcendentals=24 * tile * hidden
        ),
        name="pair_grads",
    )(core, ids_s, ids, left, right_o, right_m, right_p, targets, bias, wmt, wf)


def send_kernel(blocks, live, targets_ref, out_ref, acc):
    tile = out_ref.shape[1]
    acc[...] = jnp.zeros_like(acc)
    lane = lax.broadcasted_iota(jnp.int32, (1, tile), 1)
    counters = (lane == 0) | (lane == PANEL + 1) | (lane == 2 * (PANEL + 1))

    def slot(i, carry):
        row = blocks[i, 0]
        step = blocks[i, 1] - row
        side = jnp.where((row & 1) == 0, step, -step) + 1
        to = row * 3 + side
        for rt in range(8):
            value = targets_ref[pl.ds(i, 1), rt * tile : (rt + 1) * tile]
            if rt == 0:
                value = jnp.where(counters & (side == 1), 0.0, value)
            acc[to, rt : rt + 1, :] += value
        acc[row * 3 + 1, 0:1, :] += jnp.where(lane == side * (PANEL + 1), 1.0, 0.0)
        return carry

    lax.fori_loop(0, live[0, 0], slot, 0)
    for p in range(acc.shape[0]):
        out_ref[p * 8 : (p + 1) * 8, :] = acc[p].astype(BF)


def send_targets(blocks, live, targets, panels):
    tile = ROWS * PANEL
    smem = pl.BlockSpec(memory_space=pltpu.SMEM)
    vmem = pl.BlockSpec(memory_space=pltpu.VMEM)
    return pl.pallas_call(
        send_kernel,
        out_shape=jax.ShapeDtypeStruct((24 * panels, tile), BF),
        in_specs=[smem, smem, vmem],
        out_specs=vmem,
        scratch_shapes=[pltpu.VMEM((3 * panels, 8, tile), F32)],
        compiler_params=pltpu.CompilerParams(vmem_limit_bytes=8 << 20),
        name="send_targets",
    )(blocks, live, targets)


ORDER = (0, 1, 3, 2)


def finish_kernel(scale, pos, *refs):
    pieces, (left_ref, right_ref, mid_ref, bias_ref, fin_ref, whole) = refs[:8], refs[8:]
    part = whole.shape[2] // 4
    depth = whole.shape[2] - 128
    block = left_ref.shape[0]

    @pl.when(pl.program_id(0) == 0)
    def _():
        for n, ref in enumerate(pieces):
            side = pos[0] if n < 4 else 1 - pos[0]
            column = lax.rem(pos[1] - ORDER[n % 4] + 4, 4)
            for m, dy in enumerate(ORDER):
                row = pl.multiple_of(lax.rem(pos[2] - dy + 4, 4) * part, 32)
                whole[side, column, pl.ds(row, part), :] = ref[m * part : (m + 1) * part, :]
        for j in range(4):
            lanes = slice(j * 128, (j + 1) * 128)
            mid_ref[lanes, :] = whole[0, j, depth : depth + 128, :].astype(F32) * scale
            bias_ref[:, lanes] = whole[1, j, depth : depth + 1, :].astype(F32) * scale
        fin_ref[...] = whole[1, 0, depth + 16 : depth + 17, :].astype(F32) * scale

    rows = pl.ds(pl.multiple_of(pl.program_id(0) * block, block), block)
    for j in range(4):
        lanes = slice(j * 128, (j + 1) * 128)
        left_ref[:, lanes] = whole[0, j, rows, :].astype(F32) * scale
        right_ref[:, lanes] = whole[1, j, rows, :].astype(F32) * scale


def local(
    embeddings,
    cluster_ids,
    block_list,
    block_counts,
    pair_targets,
    w_left,
    w_right,
    hidden_bias,
    w_middle,
    w_final,
):
    emb = embeddings[0]
    depth = emb.shape[1]
    hidden = w_left.shape[1]
    upper = w_middle.shape[1]
    panels = lax.axis_size("blk")
    groups = lax.axis_size("grp")
    me = lax.axis_index("blk")
    core, x, y = me & 1, (me >> 1) & 3, me >> 3

    def blk(value, partner):
        return lax.ppermute(value, "blk", [(i, partner(i)) for i in range(panels)])

    def on_core(value):
        return blk(value, lambda i: i ^ 1)

    def on_outer(value):
        return blk(value, lambda i: (i - 1 if i % 2 == 0 else i + 1) % panels)

    def on_x(value, d):
        return blk(value, lambda i: i // 8 * 8 + (i // 2 % 4 + d) % 4 * 2 + i % 2)

    def on_y(value, d):
        return blk(value, lambda i: (i // 8 + d) % 4 * 8 + i % 8)

    def on_z(value, d):
        return lax.ppermute(value, "grp", [(i, (i + d) % groups) for i in range(groups)])

    sums = send_targets(block_list[0], block_counts, pair_targets[0], panels).reshape(panels, 24, ROWS * PANEL)
    sums, emb, ids = lax.optimization_barrier((sums, emb, cluster_ids[0]))
    with jax.named_scope("to_owner"):
        targets = lax.all_to_all(sums, "blk", 0, 0, tiled=True)
    targets = targets.reshape(24 * panels, ROWS * PANEL)

    left = jnp.dot(emb, w_left, preferred_element_type=F32).astype(BF)
    right = jnp.dot(emb, w_right, preferred_element_type=F32).astype(BF)
    ids = ids.astype(BF)
    ids_row = jnp.pad(ids[None, :], ((0, 15), (0, hidden - PANEL)))
    right_own = jnp.concatenate([right, ids_row], axis=0)
    right_outer = on_outer(right_own)
    right_partner = on_core(right_own)
    col_ids = jnp.stack([right_outer[PANEL, :PANEL], ids, right_partner[PANEL, :PANEL]])
    lg, r_outer, r_own, keep, sent = pair_grads(
        core[None],
        col_ids.astype(jnp.int32),
        jnp.pad(col_ids.astype(F32), ((0, 5), (0, 0))),
        left,
        right_outer,
        right_own,
        right_partner,
        targets,
        hidden_bias[None, :],
        w_middle.T,
        w_final[:, None],
    )

    emb_pair = jnp.concatenate([emb, on_core(emb)], axis=0)
    emb_all = jnp.concatenate([emb_pair] + [on_x(emb_pair, d) for d in ORDER[1:]], axis=0)

    first = core == 0
    got = on_core(sent)
    outer = on_outer(r_outer).astype(F32)
    over = lax.ppermute(r_outer, "blk", [(i, (i + 2) % panels) for i in range(1, panels, 2)]).astype(F32)
    r_partner = sent[PANEL : 2 * PANEL].astype(F32)
    rg = (r_own.astype(F32) + got[PANEL : 2 * PANEL].astype(F32) + outer).astype(BF)
    pair_right = (got[:PANEL].astype(F32) + r_partner + over).astype(BF)
    extra = keep.astype(F32) + got[2 * PANEL :].astype(F32)
    both = jnp.concatenate(
        [jnp.where(first, lg, rg), jnp.where(first, got[:PANEL], pair_right), extra.astype(BF)], axis=0
    )
    grad_local = jnp.dot(lg, w_left.T, preferred_element_type=F32) + jnp.dot(
        rg, w_right.T, preferred_element_type=F32
    )

    def column(d):
        return lax.dynamic_slice_in_dim(both, ((x + d) & 3) * 128, 128, 1)

    parts = [column(0)] + [on_x(column(d), d) for d in ORDER[1:]]
    grads = jnp.concatenate([p[: 2 * PANEL] for p in parts], axis=0)
    weight = lax.dot_general(emb_all, grads, (((0,), (0,)), ((), ())), preferred_element_type=F32)
    extra = sum(p[2 * PANEL :].astype(F32) for p in parts)
    total = jnp.concatenate([weight, extra], axis=0).astype(BF)
    piece = total.shape[0] // 4

    def rows(d):
        return lax.dynamic_slice_in_dim(total, ((y + d) & 3) * piece, piece, 0)

    parts = [rows(0)] + [on_y(rows(d), d) for d in ORDER[1:]]
    total = sum(p.astype(F32) for p in parts).astype(BF)
    total = (
        total.astype(F32)
        + lax.ppermute(total, "grp", [(i, i ^ 1) for i in range(groups)]).astype(F32)
    ).astype(BF)
    total = sum(p.astype(F32) for p in [total] + [on_z(total, d) for d in (2, 6, 4)]).astype(BF)

    total = jnp.concatenate([total] + [on_y(total, d) for d in ORDER[1:]], axis=0)
    mine = [total] + [on_x(total, d) for d in ORDER[1:]]
    theirs = [on_core(p) for p in mine]
    devices = panels * groups
    scale = 1.0 / math.sqrt(devices * B_DEV * PANEL)
    vmem = pl.BlockSpec(memory_space=pltpu.VMEM)
    block = depth // 4
    grad_left, grad_right, grad_middle, grad_bias, grad_final = pl.pallas_call(
        lambda *refs: finish_kernel(scale, *refs),
        grid=(4,),
        out_shape=(
            jax.ShapeDtypeStruct((depth, hidden), F32),
            jax.ShapeDtypeStruct((depth, hidden), F32),
            jax.ShapeDtypeStruct((hidden, upper), F32),
            jax.ShapeDtypeStruct((1, hidden), F32),
            jax.ShapeDtypeStruct((1, upper), F32),
        ),
        in_specs=[pl.BlockSpec(memory_space=pltpu.SMEM)] + [vmem] * 8,
        out_specs=(
            pl.BlockSpec((block, hidden), lambda i: (i, 0)),
            pl.BlockSpec((block, hidden), lambda i: (i, 0)),
            pl.BlockSpec((hidden, upper), lambda i: (0, 0)),
            pl.BlockSpec((1, hidden), lambda i: (0, 0)),
            pl.BlockSpec((1, upper), lambda i: (0, 0)),
        ),
        scratch_shapes=[pltpu.VMEM((2, 4, 4 * piece, 128), BF)],
        compiler_params=pltpu.CompilerParams(vmem_limit_bytes=16 << 20),
        name="finish",
    )(jnp.stack([core, x, y]), *mine, *theirs)
    return (grad_local[None], grad_left, grad_right, grad_bias[0], grad_middle, grad_final[0])


def solution(mesh):
    return jax.shard_map(
        local,
        mesh=mesh,
        in_specs=(
            P("grp", "blk", None),
            P("grp", "blk"),
            P("grp", "blk", None),
            P("grp", "blk"),
            P("grp", "blk", None),
            P(),
            P(),
            P(),
            P(),
            P(),
        ),
        out_specs=(P("grp", "blk", None), P(), P(), P(), P(), P()),
        check_vma=False,
    )
```

```python
import math

import jax
import jax.numpy as jnp
from jax import lax
from jax.experimental import pallas as pl
from jax.experimental.pallas import tpu as pltpu
from jax.sharding import PartitionSpec as P

PANEL = 64
B_DEV = 8
ROWS = 8
CHUNK = 256
BF = jnp.bfloat16
F32 = jnp.float32


def list_tiles(ids_s, todo):
    def scan(i, n):
        k, rt = i // 8, i % 8
        meets = (ids_s[1, rt * ROWS] <= ids_s[k, PANEL - 1]) & (ids_s[k, 0] <= ids_s[1, rt * ROWS + ROWS - 1])
        todo[n] = i
        return n + meets.astype(jnp.int32)

    return lax.fori_loop(0, 24, scan, 0)


def halve(left_ref, bias_ref, rights, left_s, right_s):
    left_s[...] = (left_ref[...].astype(F32) + bias_ref[...]) * 0.5
    for k, ref in enumerate(rights):
        right_s[k * PANEL : (k + 1) * PANEL, :] = (ref[0:PANEL, :].astype(F32) * 0.5).astype(BF)


def hidden_layer(tile_at, left_s, right_s, hid_s, slope_s=None):
    left8 = left_s[pl.ds(pl.multiple_of(tile_at % 8 * ROWS, ROWS), ROWS), :]
    right = right_s[pl.ds(pl.multiple_of(tile_at // 8 * PANEL, PANEL), PANEL), :]
    for a in range(ROWS):
        part = slice(a * PANEL, (a + 1) * PANEL)
        u = right + jnp.broadcast_to(left8[a : a + 1, :], right.shape).astype(BF)
        p = jnp.tanh(u) + BF(1.0)
        h = u * p
        hid_s[part, :] = h
        if slope_s is not None:
            slope_s[part, :] = p + h * (BF(2.0) - p)


def forward_kernel(
    ids_s, ids_ref, left_ref, right_o, right_m, right_p, bias_ref, wm_ref, wf_ref, kept_ref, rows_ref,
    todo, left_s, right_s, half_s, hid_s, mask_s, kept_s, rows_s, sems,
):
    tile = ROWS * PANEL
    iota = lambda shape, axis: lax.broadcasted_iota(jnp.int32, shape, axis)
    n_todo = list_tiles(ids_s, todo)
    halve(left_ref, bias_ref, (right_o, right_m, right_p), left_s, right_s)
    half_s[...] = (wm_ref[...].astype(F32) * 0.5).astype(BF)
    ids = ids_ref[...]
    spread = (iota((PANEL, tile), 0) % ROWS == iota((PANEL, tile), 1) // PANEL).astype(BF)
    repeat = (iota((PANEL, tile), 0) == iota((PANEL, tile), 1) % PANEL).astype(BF)
    row_ids = jnp.where(iota((8, PANEL), 1) // ROWS == iota((8, PANEL), 0), ids[1:2, :], 0.0)
    row_ids = jnp.dot(row_ids.astype(BF), spread, preferred_element_type=F32)
    col_ids = jnp.dot(ids.astype(BF), repeat, preferred_element_type=F32)
    lane = iota((8, tile), 1)
    itself = iota((8, tile), 0) * ROWS + lane // PANEL == lane % PANEL
    for k in range(3):
        same = row_ids == col_ids[k : k + 1, :]
        mask = jnp.where(same & ~itself if k == 1 else same, 16.0, 0.0)
        for rt in range(8):
            mask_s[k * 8 + rt, 0:1, :] = mask[rt : rt + 1, :]

    def put(i):
        return (
            pltpu.make_async_copy(kept_s.at[i & 1], kept_ref.at[todo[i]], sems.at[0, i & 1]),
            pltpu.make_async_copy(rows_s.at[i & 1], rows_ref.at[todo[i]], sems.at[1, i & 1]),
        )

    def step(i, carry):
        tile_at = todo[i]
        hidden_layer(tile_at, left_s, right_s, hid_s)

        @pl.when(i >= 2)
        def _():
            for copy in put(i - 2):
                copy.wait()

        wf = wf_ref[...]
        upper = wf.shape[0]
        rows_s[i & 1, 1:2, :] = mask_s[tile_at, 0:1, :]
        for c in range(tile // CHUNK):
            part = slice(c * CHUNK, (c + 1) * CHUNK)
            u = jnp.dot(hid_s[part, :], half_s[...], preferred_element_type=F32).T
            p = jnp.tanh(u) + 1.0
            act = u * p
            rows_s[i & 1, 0:1, part] = jnp.sum(act * wf, axis=0, keepdims=True)
            kept_s[i & 1, 0:upper, part] = ((0.5 * wf) * (p + act * (2.0 - p))).astype(BF)
            kept_s[i & 1, upper:, part] = act.astype(BF)
        for copy in put(i):
            copy.start()
        return carry

    lax.fori_loop(0, n_todo, step, 0)

    def drain(i, carry):
        for copy in put(i):
            copy.wait()
        return carry

    lax.fori_loop(jnp.maximum(n_todo - 2, 0), n_todo, drain, 0)


def backward_kernel(
    core, ids_s, left_ref, right_o, right_m, right_p, kept_ref, rows_ref, targets_ref, bias_ref, wmt_ref,
    out_left, out_outer, out_own, out_keep, out_sent,
    todo, left_s, right_s, tsum_s, hid_s, slope_s, lacc, racc, mid_acc, fin_acc, kept_s, rows_s, sems,
):
    hidden = left_ref.shape[1]
    tile = ROWS * PANEL
    iota = lambda shape, axis: lax.broadcasted_iota(jnp.int32, shape, axis)
    n_todo = list_tiles(ids_s, todo)

    def fetch(i):
        return (
            pltpu.make_async_copy(kept_ref.at[todo[i]], kept_s.at[i & 1], sems.at[0, i & 1]),
            pltpu.make_async_copy(rows_ref.at[todo[i]], rows_s.at[i & 1], sems.at[1, i & 1]),
        )

    @pl.when(n_todo > 0)
    def _():
        for copy in fetch(0):
            copy.start()

    halve(left_ref, bias_ref, (right_o, right_m, right_p), left_s, right_s)
    n_src = targets_ref.shape[0]
    tsum = jnp.dot(
        (iota((24, n_src), 1) % 24 == iota((24, n_src), 0)).astype(BF), targets_ref[...], preferred_element_type=F32
    )
    for k in range(3):
        count = jnp.max(
            jnp.where(iota((1, tile), 1) == k * (PANEL + 1), tsum[8:9, :], 0.0), axis=1, keepdims=True
        )
        tsum_s[24 + k, 0:1, :] = jnp.broadcast_to(count, (1, tile))
    for i in range(24):
        tsum_s[i, 0:1, :] = tsum[i : i + 1, :]
    lacc[...] = jnp.zeros_like(lacc)
    racc[...] = jnp.zeros_like(racc)
    mid_acc[...] = jnp.zeros_like(mid_acc)
    fin_acc[...] = jnp.zeros_like(fin_acc)

    def step(i, carry):
        tile_at = todo[i]
        col0 = pl.multiple_of(tile_at // 8 * PANEL, PANEL)
        row0 = pl.multiple_of(tile_at % 8 * ROWS, ROWS)

        @pl.when(i + 1 < n_todo)
        def _():
            for copy in fetch(i + 1):
                copy.start()

        for copy in fetch(i):
            copy.wait()
        slope = rows_s[i & 1, 1:2, :] * (
            tsum_s[tile_at // 8 + 24, 0:1, :] * rows_s[i & 1, 0:1, :] - tsum_s[tile_at, 0:1, :]
        )
        upper = wmt_ref.shape[0]
        seconds, hiddens, fins = [], [], []
        parts = [slice(c * CHUNK, (c + 1) * CHUNK) for c in range(tile // CHUNK)]
        for part in parts:
            seconds.append((kept_s[i & 1, 0:upper, part].astype(F32) * slope[:, part]).astype(BF))
            hiddens.append(
                lax.dot_general(seconds[-1], wmt_ref[...], (((0,), (0,)), ((), ())), preferred_element_type=F32)
            )
            fin = kept_s[i & 1, upper:, part].astype(F32) * slope[:, part]
            fins.append(sum(fin[:, j * 128 : (j + 1) * 128] for j in range(CHUNK // 128)))
        fin_acc[...] += sum(fins)
        hidden_layer(tile_at, left_s, right_s, hid_s, slope_s)
        terms = [jnp.dot(g, hid_s[part, :], preferred_element_type=F32) for g, part in zip(seconds, parts)]
        cols, rows = None, []
        for part, grad_hidden in zip(parts, hiddens):
            for a in range(CHUNK // PANEL):
                at = slice(part.start + a * PANEL, part.start + (a + 1) * PANEL)
                g = grad_hidden[a * PANEL : (a + 1) * PANEL, :] * slope_s[at, :].astype(F32)
                rows.append(jnp.sum(g, axis=0, keepdims=True))
                cols = g if cols is None else cols + g
        mid_acc[...] += sum(terms)
        racc[pl.ds(col0, PANEL), :] += cols
        lacc[pl.ds(row0, ROWS), :] += jnp.concatenate(rows, axis=0)
        return carry

    lax.fori_loop(0, n_todo, step, 0)
    left = lacc[...] * 0.5
    out_left[...] = left.astype(BF)
    outer, own, partner = [
        (racc[k * PANEL : (k + 1) * PANEL, :] * 0.5).astype(BF) for k in range(3)
    ]
    out_outer[...] = outer
    out_own[...] = own
    out_sent[PANEL : 2 * PANEL, :] = partner

    def middle(ref, start):
        for j in range(hidden // 128):
            block = slice(j * 128, (j + 1) * 128)
            ref[start : start + 128, block] = mid_acc[:, block].T.astype(BF)

    def small(ref, start):
        ref[start : start + 128, :] = jnp.zeros((128, hidden), BF)
        ref[start : start + 1, :] = jnp.sum(left, axis=0, keepdims=True).astype(BF)
        ref[start + 16 : start + 17, 0:128] = jnp.sum(fin_acc[...].T, axis=0, keepdims=True).astype(BF)

    @pl.when(core[0] == 0)
    def _():
        out_sent[0:PANEL, :] = own
        small(out_sent, 2 * PANEL)
        middle(out_keep, 0)

    @pl.when(core[0] != 0)
    def _():
        out_sent[0:PANEL, :] = left.astype(BF)
        middle(out_sent, 2 * PANEL)
        small(out_keep, 0)


def pair_forward(ids_s, ids, left, rights, bias, wm, wf):
    hidden, upper = wm.shape
    tile = ROWS * PANEL
    vmem = pl.BlockSpec(memory_space=pltpu.VMEM)
    return pl.pallas_call(
        forward_kernel,
        out_shape=(
            pltpu.HBM((24, 2 * upper, tile), BF),
            pltpu.HBM((24, 8, tile), F32),
        ),
        in_specs=[pl.BlockSpec(memory_space=pltpu.SMEM)] + [vmem] * 8,
        out_specs=(pl.BlockSpec(memory_space=pltpu.HBM),) * 2,
        scratch_shapes=[
            pltpu.SMEM((32,), jnp.int32),
            pltpu.VMEM((PANEL, hidden), F32),
            pltpu.VMEM((3 * PANEL, hidden), BF),
            pltpu.VMEM((hidden, upper), BF),
            pltpu.VMEM((tile, hidden), BF),
            pltpu.VMEM((24, 8, tile), F32),
            pltpu.VMEM((2, 2 * upper, tile), BF),
            pltpu.VMEM((2, 8, tile), F32),
            pltpu.SemaphoreType.DMA((2, 2)),
        ],
        compiler_params=pltpu.CompilerParams(vmem_limit_bytes=12 << 20),
        cost_estimate=pl.CostEstimate(
            flops=2 * 24 * tile * hidden * upper, bytes_accessed=8 << 20, transcendentals=24 * tile * hidden
        ),
        name="pair_forward",
    )(ids_s, ids, left, *rights, bias, wm, wf)


def pair_backward(core, ids_s, left, rights, kept, targets, bias, wmt):
    hidden = left.shape[1]
    upper = wmt.shape[0]
    tile = ROWS * PANEL
    vmem = pl.BlockSpec(memory_space=pltpu.VMEM)
    panel = jax.ShapeDtypeStruct((PANEL, hidden), BF)
    return pl.pallas_call(
        backward_kernel,
        out_shape=(
            panel,
            panel,
            panel,
            jax.ShapeDtypeStruct((upper, hidden), BF),
            jax.ShapeDtypeStruct((2 * PANEL + upper, hidden), BF),
        ),
        in_specs=[pl.BlockSpec(memory_space=pltpu.SMEM)] * 2
        + [vmem] * 4
        + [pl.BlockSpec(memory_space=pltpu.HBM)] * 2
        + [vmem] * 3,
        out_specs=(vmem,) * 5,
        scratch_shapes=[
            pltpu.SMEM((32,), jnp.int32),
            pltpu.VMEM((PANEL, hidden), F32),
            pltpu.VMEM((3 * PANEL, hidden), BF),
            pltpu.VMEM((27, 8, tile), F32),
            pltpu.VMEM((tile, hidden), BF),
            pltpu.VMEM((tile, hidden), BF),
            pltpu.VMEM((PANEL, hidden), F32),
            pltpu.VMEM((3 * PANEL, hidden), F32),
            pltpu.VMEM((upper, hidden), F32),
            pltpu.VMEM((upper, 128), F32),
            pltpu.VMEM((2, 2 * upper, tile), BF),
            pltpu.VMEM((2, 8, tile), F32),
            pltpu.SemaphoreType.DMA((2, 2)),
        ],
        compiler_params=pltpu.CompilerParams(vmem_limit_bytes=12 << 20),
        cost_estimate=pl.CostEstimate(
            flops=4 * 24 * tile * hidden * upper, bytes_accessed=8 << 20, transcendentals=24 * tile * hidden
        ),
        name="pair_backward",
    )(core, ids_s, left, *rights, *kept, targets, bias, wmt)


def send_kernel(blocks, live, targets_ref, out_ref, acc):
    tile = out_ref.shape[1]
    acc[...] = jnp.zeros_like(acc)
    lane = lax.broadcasted_iota(jnp.int32, (1, tile), 1)
    counters = (lane == 0) | (lane == PANEL + 1) | (lane == 2 * (PANEL + 1))

    def slot(i, carry):
        row = blocks[i, 0]
        step = blocks[i, 1] - row
        side = jnp.where((row & 1) == 0, step, -step) + 1
        to = row * 3 + side
        for rt in range(8):
            value = targets_ref[pl.ds(i, 1), rt * tile : (rt + 1) * tile]
            if rt == 0:
                value = jnp.where(counters & (side == 1), 0.0, value)
            acc[to, rt : rt + 1, :] += value
        acc[row * 3 + 1, 0:1, :] += jnp.where(lane == side * (PANEL + 1), 1.0, 0.0)
        return carry

    lax.fori_loop(0, live[0, 0], slot, 0)
    for p in range(acc.shape[0]):
        out_ref[p * 8 : (p + 1) * 8, :] = acc[p].astype(BF)


def send_targets(blocks, live, targets, panels):
    tile = ROWS * PANEL
    smem = pl.BlockSpec(memory_space=pltpu.SMEM)
    vmem = pl.BlockSpec(memory_space=pltpu.VMEM)
    return pl.pallas_call(
        send_kernel,
        out_shape=jax.ShapeDtypeStruct((24 * panels, tile), BF),
        in_specs=[smem, smem, vmem],
        out_specs=vmem,
        scratch_shapes=[pltpu.VMEM((3 * panels, 8, tile), F32)],
        compiler_params=pltpu.CompilerParams(vmem_limit_bytes=8 << 20),
        name="send_targets",
    )(blocks, live, targets)


def slice_kernel(*refs):
    embs, parts, out = refs[:4], refs[4:8], refs[8]
    depth = embs[0].shape[1]
    rows = embs[0].shape[0]
    total = extra = None
    for emb, part in zip(embs, parts):
        term = lax.dot_general(
            emb[...], part[0:rows, :], (((0,), (0,)), ((), ())), preferred_element_type=F32
        )
        more = part[rows:, :].astype(F32)
        total = term if total is None else total + term
        extra = more if extra is None else extra + more
    out[0:depth, :] = total.astype(BF)
    out[depth:, :] = extra.astype(BF)


def weight_slice(embs, parts):
    rows, depth = embs[0].shape
    vmem = pl.BlockSpec(memory_space=pltpu.VMEM)
    return pl.pallas_call(
        slice_kernel,
        out_shape=jax.ShapeDtypeStruct((depth + parts[0].shape[0] - rows, parts[0].shape[1]), BF),
        in_specs=[vmem] * 8,
        out_specs=vmem,
        compiler_params=pltpu.CompilerParams(vmem_limit_bytes=16 << 20),
        name="weight_slice",
    )(*embs, *parts)


ORDER = (0, 1, 3, 2)


def finish_kernel(scale, pos, *refs):
    pieces, (left_ref, right_ref, mid_ref, bias_ref, fin_ref, whole) = refs[:8], refs[8:]
    part = whole.shape[2] // 4
    depth = whole.shape[2] - 128
    block = left_ref.shape[0]

    @pl.when(pl.program_id(0) == 0)
    def _():
        for n, ref in enumerate(pieces):
            side = pos[0] if n < 4 else 1 - pos[0]
            column = lax.rem(pos[1] - ORDER[n % 4] + 4, 4)
            for m, dy in enumerate(ORDER):
                row = pl.multiple_of(lax.rem(pos[2] - dy + 4, 4) * part, 32)
                whole[side, column, pl.ds(row, part), :] = ref[m * part : (m + 1) * part, :]
        for j in range(4):
            lanes = slice(j * 128, (j + 1) * 128)
            mid_ref[lanes, :] = whole[0, j, depth : depth + 128, :].astype(F32) * scale
            bias_ref[:, lanes] = whole[1, j, depth : depth + 1, :].astype(F32) * scale
        fin_ref[...] = whole[1, 0, depth + 16 : depth + 17, :].astype(F32) * scale

    rows = pl.ds(pl.multiple_of(pl.program_id(0) * block, block), block)
    for j in range(4):
        lanes = slice(j * 128, (j + 1) * 128)
        left_ref[:, lanes] = whole[0, j, rows, :].astype(F32) * scale
        right_ref[:, lanes] = whole[1, j, rows, :].astype(F32) * scale


def local(
    embeddings,
    cluster_ids,
    block_list,
    block_counts,
    pair_targets,
    w_left,
    w_right,
    hidden_bias,
    w_middle,
    w_final,
):
    emb = embeddings[0]
    depth = emb.shape[1]
    hidden = w_left.shape[1]
    upper = w_middle.shape[1]
    panels = lax.axis_size("blk")
    groups = lax.axis_size("grp")
    me = lax.axis_index("blk")
    core, x, y = me & 1, (me >> 1) & 3, me >> 3

    def blk(value, partner):
        return lax.ppermute(value, "blk", [(i, partner(i)) for i in range(panels)])

    def on_core(value):
        return blk(value, lambda i: i ^ 1)

    def on_outer(value):
        return blk(value, lambda i: (i - 1 if i % 2 == 0 else i + 1) % panels)

    def on_x(value, d):
        return blk(value, lambda i: i // 8 * 8 + (i // 2 % 4 + d) % 4 * 2 + i % 2)

    def on_y(value, d):
        return blk(value, lambda i: (i // 8 + d) % 4 * 8 + i % 8)

    def on_z(value, d):
        return lax.ppermute(value, "grp", [(i, (i + d) % groups) for i in range(groups)])

    right = jnp.dot(emb, w_right, preferred_element_type=F32).astype(BF)
    ids = cluster_ids[0].astype(BF)
    ids_row = jnp.pad(ids[None, :], ((0, 15), (0, hidden - PANEL)))
    right_own = jnp.concatenate([right, ids_row], axis=0)
    right_outer = on_outer(right_own)
    right_partner = on_core(right_own)

    sums = send_targets(block_list[0], block_counts, pair_targets[0], panels).reshape(panels, 24, ROWS * PANEL)
    targets = lax.all_to_all(sums, "blk", 0, 0, tiled=True)
    targets = targets.reshape(24 * panels, ROWS * PANEL)

    left = jnp.dot(emb, w_left, preferred_element_type=F32).astype(BF)
    col_ids = jnp.stack([right_outer[PANEL, :PANEL], ids, right_partner[PANEL, :PANEL]])
    ids_s = col_ids.astype(jnp.int32)
    rights = (right_outer, right_own, right_partner)
    kept = pair_forward(
        ids_s,
        jnp.pad(col_ids.astype(F32), ((0, 5), (0, 0))),
        left,
        rights,
        hidden_bias[None, :],
        w_middle,
        w_final[:, None],
    )

    kept = [pltpu.with_memory_space_constraint(k, pltpu.HBM) for k in kept]

    emb_pair = jnp.concatenate([emb, on_core(emb)], axis=0)
    embs = [emb_pair]
    for d in ORDER[1:]:
        embs.append(on_x(emb_pair, d))

    lg, r_outer, r_own, keep, sent = pair_backward(
        core[None], ids_s, left, rights, kept, targets, hidden_bias[None, :], w_middle.T
    )

    first = core == 0
    got = on_core(sent)
    outer = on_outer(r_outer).astype(F32)
    over = lax.ppermute(r_outer, "blk", [(i, (i + 2) % panels) for i in range(1, panels, 2)]).astype(F32)
    r_partner = sent[PANEL : 2 * PANEL].astype(F32)
    rg = (r_own.astype(F32) + got[PANEL : 2 * PANEL].astype(F32) + outer).astype(BF)
    pair_right = (got[:PANEL].astype(F32) + r_partner + over).astype(BF)
    extra = keep.astype(F32) + got[2 * PANEL :].astype(F32)
    both = jnp.concatenate(
        [jnp.where(first, lg, rg), jnp.where(first, got[:PANEL], pair_right), extra.astype(BF)], axis=0
    )
    grad_local = jnp.dot(lg, w_left.T, preferred_element_type=F32) + jnp.dot(
        rg, w_right.T, preferred_element_type=F32
    )

    def column(d):
        return lax.dynamic_slice_in_dim(both, ((x + d) & 3) * 128, 128, 1)

    parts = [column(0)] + [on_x(column(d), d) for d in ORDER[1:]]
    total = weight_slice(embs, parts)
    piece = total.shape[0] // 4

    def rows(d):
        return lax.dynamic_slice_in_dim(total, ((y + d) & 3) * piece, piece, 0)

    parts = [rows(0)] + [on_y(rows(d), d) for d in ORDER[1:]]
    total = sum(p.astype(F32) for p in parts).astype(BF)
    total = (
        total.astype(F32)
        + lax.ppermute(total, "grp", [(i, i ^ 1) for i in range(groups)]).astype(F32)
    ).astype(BF)
    total = sum(p.astype(F32) for p in [total] + [on_z(total, d) for d in (2, 6, 4)]).astype(BF)
    total, grad_local = lax.optimization_barrier((total, grad_local))

    total = jnp.concatenate([total] + [on_y(total, d) for d in ORDER[1:]], axis=0)
    mine = [total] + [on_x(total, d) for d in ORDER[1:]]
    theirs = [on_core(p) for p in mine]
    devices = panels * groups
    scale = 1.0 / math.sqrt(devices * B_DEV * PANEL)
    vmem = pl.BlockSpec(memory_space=pltpu.VMEM)
    block = depth // 4
    grad_left, grad_right, grad_middle, grad_bias, grad_final = pl.pallas_call(
        lambda *refs: finish_kernel(scale, *refs),
        grid=(4,),
        out_shape=(
            jax.ShapeDtypeStruct((depth, hidden), F32),
            jax.ShapeDtypeStruct((depth, hidden), F32),
            jax.ShapeDtypeStruct((hidden, upper), F32),
            jax.ShapeDtypeStruct((1, hidden), F32),
            jax.ShapeDtypeStruct((1, upper), F32),
        ),
        in_specs=[pl.BlockSpec(memory_space=pltpu.SMEM)] + [vmem] * 8,
        out_specs=(
            pl.BlockSpec((block, hidden), lambda i: (i, 0)),
            pl.BlockSpec((block, hidden), lambda i: (i, 0)),
            pl.BlockSpec((hidden, upper), lambda i: (0, 0)),
            pl.BlockSpec((1, hidden), lambda i: (0, 0)),
            pl.BlockSpec((1, upper), lambda i: (0, 0)),
        ),
        scratch_shapes=[pltpu.VMEM((2, 4, 4 * piece, 128), BF)],
        compiler_params=pltpu.CompilerParams(vmem_limit_bytes=16 << 20),
        name="finish",
    )(jnp.stack([core, x, y]), *mine, *theirs)
    return (grad_local[None], grad_left, grad_right, grad_bias[0], grad_middle, grad_final[0])


def solution(mesh):
    return jax.shard_map(
        local,
        mesh=mesh,
        in_specs=(
            P("grp", "blk", None),
            P("grp", "blk"),
            P("grp", "blk", None),
            P("grp", "blk"),
            P("grp", "blk", None),
            P(),
            P(),
            P(),
            P(),
            P(),
        ),
        out_specs=(P("grp", "blk", None), P(), P(), P(), P(), P()),
        check_vma=False,
    )
```

```python
import math

import jax
import jax.numpy as jnp
from jax import lax
from jax.experimental import pallas as pl
from jax.experimental.pallas import tpu as pltpu
from jax.sharding import PartitionSpec as P

PANEL = 64
B_DEV = 8
ROWS = 8
CHUNK = 256
BF = jnp.bfloat16
F32 = jnp.float32


def forward(tile_at, left_s, right_s, hid_s, slope_s, rows=range(ROWS)):
    k = tile_at // 8
    left8 = left_s[pl.ds(pl.multiple_of(tile_at % 8 * ROWS, ROWS), ROWS), :]
    right = right_s[pl.ds(pl.multiple_of(k * PANEL, PANEL), PANEL), :]
    for a in rows:
        part = slice(a * PANEL, (a + 1) * PANEL)
        u = right.astype(BF) + jnp.broadcast_to(left8[a : a + 1, :], right.shape).astype(BF)
        p = jnp.tanh(u) + BF(1.0)
        h = u * p
        hid_s[part, :] = h
        slope_s[part, :] = p + h * (BF(2.0) - p)


def backward(
    tile_at, hid_s, slope_s, tsum_s, mask_s, half_s, wmt_ref, wf_ref, lacc, racc, mid_acc, fin_acc
):
    col0 = pl.multiple_of(tile_at // 8 * PANEL, PANEL)
    row0 = pl.multiple_of(tile_at % 8 * ROWS, ROWS)
    wf = wf_ref[...]
    count = tsum_s[tile_at // 8 * 8 + 24, 0:1, 0:CHUNK]
    parts = [slice(c * CHUNK, (c + 1) * CHUNK) for c in range(ROWS * PANEL // CHUNK)]
    pre = [
        jnp.dot(hid_s[part, :], half_s[...], preferred_element_type=F32).T
        for part in parts
    ]
    terms, hiddens, fins = [], [], []
    for part, u in zip(parts, pre):
        p = jnp.tanh(u) + 1.0
        act = u * p
        predicted = jnp.sum(act * wf, axis=0, keepdims=True)
        pair_slope = (16.0 * mask_s[tile_at, 0:1, part]) * (count * predicted - tsum_s[tile_at, 0:1, part])
        grad_second = ((0.5 * pair_slope) * wf * (p + act * (2.0 - p))).astype(BF)
        fin = act * pair_slope
        fins.append(sum(fin[:, j * 128 : (j + 1) * 128] for j in range(CHUNK // 128)))
        hiddens.append(
            lax.dot_general(grad_second, wmt_ref[...], (((0,), (0,)), ((), ())), preferred_element_type=F32)
        )
        terms.append(jnp.dot(grad_second, hid_s[part, :], preferred_element_type=F32))
    fin_acc[...] += sum(fins)
    cols, rows = None, []
    for part, grad_hidden in zip(parts, hiddens):
        for a in range(CHUNK // PANEL):
            at = slice(part.start + a * PANEL, part.start + (a + 1) * PANEL)
            g = grad_hidden[a * PANEL : (a + 1) * PANEL, :] * slope_s[at, :].astype(F32)
            rows.append(jnp.sum(g, axis=0, keepdims=True))
            cols = g if cols is None else cols + g
    mid_acc[...] += sum(terms)
    racc[pl.ds(col0, PANEL), :] += cols
    lacc[pl.ds(row0, ROWS), :] += jnp.concatenate(rows, axis=0)


def pair_kernel(
    core,
    ids_s,
    ids_ref,
    left_ref,
    right_o,
    right_m,
    right_p,
    targets_ref,
    bias_ref,
    wmt_ref,
    wf_ref,
    out_left,
    out_outer,
    out_own,
    out_keep,
    out_sent,
    todo,
    panels_s,
    sems,
    left_s,
    right_s,
    tsum_s,
    mask_s,
    half_s,
    hid_s,
    slope_s,
    lacc,
    racc,
    mid_acc,
    fin_acc,
):
    hidden = left_ref.shape[1]
    tile = ROWS * PANEL
    loads = [
        pltpu.make_async_copy(ref.at[0:PANEL, :], panels_s.at[n], sems.at[n])
        for n, ref in enumerate((left_ref, right_o, right_m, right_p))
    ]
    for copy in loads:
        copy.start()
    iota = lambda shape, axis: lax.broadcasted_iota(jnp.int32, shape, axis)

    def scan(i, n):
        k, rt = i // 8, i % 8
        meets = (ids_s[1, rt * ROWS] <= ids_s[k, PANEL - 1]) & (ids_s[k, 0] <= ids_s[1, rt * ROWS + ROWS - 1])
        todo[n] = i
        return n + meets.astype(jnp.int32)

    n_todo = lax.fori_loop(0, 24, scan, 0)
    for extra in range(3):
        todo[n_todo + extra] = 24
    half_s[...] = (wmt_ref[...].astype(F32) * 0.5).T.astype(BF)
    n_src = targets_ref.shape[0]
    tsum = jnp.dot(
        (iota((24, n_src), 1) % 24 == iota((24, n_src), 0)).astype(BF), targets_ref[...], preferred_element_type=F32
    )
    ids = ids_ref[...]
    spread = (iota((PANEL, tile), 0) % ROWS == iota((PANEL, tile), 1) // PANEL).astype(BF)
    repeat = (iota((PANEL, tile), 0) == iota((PANEL, tile), 1) % PANEL).astype(BF)
    row_ids = jnp.where(iota((8, PANEL), 1) // ROWS == iota((8, PANEL), 0), ids[1:2, :], 0.0)
    row_ids = jnp.dot(row_ids.astype(BF), spread, preferred_element_type=F32)
    col_ids = jnp.dot(ids.astype(BF), repeat, preferred_element_type=F32)
    lane = iota((8, tile), 1)
    itself = iota((8, tile), 0) * ROWS + lane // PANEL == lane % PANEL
    for k in range(3):
        same = row_ids == col_ids[k : k + 1, :]
        mask = jnp.where(same & ~itself if k == 1 else same, 1.0, 0.0)
        count = jnp.max(
            jnp.where(iota((8, tile), 1) == k * (PANEL + 1), tsum[8:16, :], 0.0)[0:1], axis=1, keepdims=True
        )
        tsum_s[24 + 8 * k, 0:1, :] = jnp.broadcast_to(count, (1, tile))
        for rt in range(8):
            mask_s[k * 8 + rt, 0:1, :] = mask[rt : rt + 1, :]
            tsum_s[k * 8 + rt, 0:1, :] = tsum[k * 8 + rt : k * 8 + rt + 1, :]
    mask_s[24, 0:1, :] = jnp.zeros((1, tile), F32)
    tsum_s[48, 0:1, :] = jnp.zeros((1, tile), F32)
    lacc[...] = jnp.zeros_like(lacc)
    racc[...] = jnp.zeros_like(racc)
    mid_acc[...] = jnp.zeros_like(mid_acc)
    fin_acc[...] = jnp.zeros_like(fin_acc)
    for copy in loads:
        copy.wait()
    left_s[...] = (panels_s[0].astype(F32) + bias_ref[...]) * 0.5
    for k in range(3):
        right_s[k * PANEL : (k + 1) * PANEL, :] = panels_s[k + 1].astype(F32) * 0.5
    rest = (tsum_s, mask_s, half_s, wmt_ref, wf_ref, lacc, racc, mid_acc, fin_acc)

    def step(i, carry):
        forward(todo[i], left_s, right_s, hid_s, slope_s)
        backward(todo[i], hid_s, slope_s, *rest)
        return carry

    lax.fori_loop(0, n_todo, step, 0)
    left = lacc[...] * 0.5
    out_left[...] = left.astype(BF)
    outer, own, partner = [
        (racc[k * PANEL : (k + 1) * PANEL, :] * 0.5).astype(BF) for k in range(3)
    ]
    out_outer[...] = outer
    out_own[...] = own
    out_sent[PANEL : 2 * PANEL, :] = partner

    def middle(ref, start):
        for j in range(hidden // 128):
            block = slice(j * 128, (j + 1) * 128)
            ref[start : start + 128, block] = mid_acc[:, block].T.astype(BF)

    def small(ref, start):
        ref[start : start + 128, :] = jnp.zeros((128, hidden), BF)
        ref[start : start + 1, :] = jnp.sum(left, axis=0, keepdims=True).astype(BF)
        ref[start + 16 : start + 17, 0:128] = jnp.sum(fin_acc[...].T, axis=0, keepdims=True).astype(BF)

    @pl.when(core[0] == 0)
    def _():
        out_sent[0:PANEL, :] = own
        small(out_sent, 2 * PANEL)
        middle(out_keep, 0)

    @pl.when(core[0] != 0)
    def _():
        out_sent[0:PANEL, :] = left.astype(BF)
        middle(out_sent, 2 * PANEL)
        small(out_keep, 0)


def pair_grads(core, ids_s, ids, left, right_o, right_m, right_p, targets, bias, wmt, wf):
    hidden = left.shape[1]
    upper = wmt.shape[0]
    tile = ROWS * PANEL
    vmem = pl.BlockSpec(memory_space=pltpu.VMEM)
    panel = jax.ShapeDtypeStruct((PANEL, hidden), BF)
    return pl.pallas_call(
        pair_kernel,
        out_shape=(
            panel,
            panel,
            panel,
            jax.ShapeDtypeStruct((upper, hidden), BF),
            jax.ShapeDtypeStruct((2 * PANEL + upper, hidden), BF),
        ),
        in_specs=[pl.BlockSpec(memory_space=pltpu.SMEM)] * 2
        + [vmem]
        + [pl.BlockSpec(memory_space=pltpu.HBM)] * 4
        + [vmem] * 4,
        out_specs=(vmem,) * 5,
        scratch_shapes=[
            pltpu.SMEM((32,), jnp.int32),
            pltpu.VMEM((4, PANEL, hidden), BF),
            pltpu.SemaphoreType.DMA((4,)),
            pltpu.VMEM((PANEL, hidden), F32),
            pltpu.VMEM((3 * PANEL, hidden), F32),
            pltpu.VMEM((49, 8, tile), F32),
            pltpu.VMEM((25, 8, tile), F32),
            pltpu.VMEM((hidden, upper), BF),
            pltpu.VMEM((tile, hidden), BF),
            pltpu.VMEM((tile, hidden), BF),
            pltpu.VMEM((PANEL, hidden), F32),
            pltpu.VMEM((4 * PANEL, hidden), F32),
            pltpu.VMEM((upper, hidden), F32),
            pltpu.VMEM((upper, 128), F32),
        ],
        compiler_params=pltpu.CompilerParams(vmem_limit_bytes=24 << 20),
        cost_estimate=pl.CostEstimate(
            flops=10 * 24 * tile * hidden * upper, bytes_accessed=2 << 20, transcendentals=24 * tile * hidden
        ),
        name="pair_grads",
    )(core, ids_s, ids, *[pltpu.with_memory_space_constraint(v, pltpu.HBM) for v in (left, right_o, right_m, right_p)], targets, bias, wmt, wf)


def send_kernel(blocks, live, targets_ref, out_ref, acc):
    tile = out_ref.shape[1]
    acc[...] = jnp.zeros_like(acc)
    lane = lax.broadcasted_iota(jnp.int32, (1, tile), 1)
    counters = (lane == 0) | (lane == PANEL + 1) | (lane == 2 * (PANEL + 1))

    def slot(i, carry):
        row = blocks[i, 0]
        step = blocks[i, 1] - row
        side = jnp.where((row & 1) == 0, step, -step) + 1
        to = row * 3 + side
        for rt in range(8):
            value = targets_ref[pl.ds(i, 1), rt * tile : (rt + 1) * tile]
            if rt == 0:
                value = jnp.where(counters & (side == 1), 0.0, value)
            acc[to, rt : rt + 1, :] += value
        acc[row * 3 + 1, 0:1, :] += jnp.where(lane == side * (PANEL + 1), 1.0, 0.0)
        return carry

    lax.fori_loop(0, live[0, 0], slot, 0)
    for p in range(acc.shape[0]):
        out_ref[p * 8 : (p + 1) * 8, :] = acc[p].astype(BF)


def send_targets(blocks, live, targets, panels):
    tile = ROWS * PANEL
    smem = pl.BlockSpec(memory_space=pltpu.SMEM)
    vmem = pl.BlockSpec(memory_space=pltpu.VMEM)
    return pl.pallas_call(
        send_kernel,
        out_shape=jax.ShapeDtypeStruct((24 * panels, tile), BF),
        in_specs=[smem, smem, vmem],
        out_specs=vmem,
        scratch_shapes=[pltpu.VMEM((3 * panels, 8, tile), F32)],
        compiler_params=pltpu.CompilerParams(vmem_limit_bytes=8 << 20),
        name="send_targets",
    )(blocks, live, targets)


def slice_kernel(*refs):
    embs, parts, out = refs[:4], refs[4:8], refs[8]
    depth = embs[0].shape[1]
    rows = embs[0].shape[0]
    total = extra = None
    for emb, part in zip(embs, parts):
        term = lax.dot_general(
            emb[...], part[0:rows, :], (((0,), (0,)), ((), ())), preferred_element_type=F32
        )
        more = part[rows:, :].astype(F32)
        total = term if total is None else total + term
        extra = more if extra is None else extra + more
    out[0:depth, :] = total.astype(BF)
    out[depth:, :] = extra.astype(BF)


def weight_slice(embs, parts):
    rows, depth = embs[0].shape
    vmem = pl.BlockSpec(memory_space=pltpu.VMEM)
    return pl.pallas_call(
        slice_kernel,
        out_shape=jax.ShapeDtypeStruct((depth + parts[0].shape[0] - rows, parts[0].shape[1]), BF),
        in_specs=[vmem] * 8,
        out_specs=vmem,
        compiler_params=pltpu.CompilerParams(vmem_limit_bytes=16 << 20),
        name="weight_slice",
    )(*embs, *parts)


ORDER = (0, 1, 3, 2)


def finish_kernel(scale, pos, *refs):
    pieces, (left_ref, right_ref, mid_ref, bias_ref, fin_ref, whole) = refs[:8], refs[8:]
    part = whole.shape[2] // 4
    depth = whole.shape[2] - 128
    block = left_ref.shape[0]

    @pl.when(pl.program_id(0) == 0)
    def _():
        for n, ref in enumerate(pieces):
            side = pos[0] if n < 4 else 1 - pos[0]
            column = lax.rem(pos[1] - ORDER[n % 4] + 4, 4)
            for m, dy in enumerate(ORDER):
                row = pl.multiple_of(lax.rem(pos[2] - dy + 4, 4) * part, 32)
                whole[side, column, pl.ds(row, part), :] = ref[m * part : (m + 1) * part, :]
        for j in range(4):
            lanes = slice(j * 128, (j + 1) * 128)
            mid_ref[lanes, :] = whole[0, j, depth : depth + 128, :].astype(F32) * scale
            bias_ref[:, lanes] = whole[1, j, depth : depth + 1, :].astype(F32) * scale
        fin_ref[...] = whole[1, 0, depth + 16 : depth + 17, :].astype(F32) * scale

    rows = pl.ds(pl.multiple_of(pl.program_id(0) * block, block), block)
    for j in range(4):
        lanes = slice(j * 128, (j + 1) * 128)
        left_ref[:, lanes] = whole[0, j, rows, :].astype(F32) * scale
        right_ref[:, lanes] = whole[1, j, rows, :].astype(F32) * scale


def local(
    embeddings,
    cluster_ids,
    block_list,
    block_counts,
    pair_targets,
    w_left,
    w_right,
    hidden_bias,
    w_middle,
    w_final,
):
    emb = embeddings[0]
    depth = emb.shape[1]
    hidden = w_left.shape[1]
    upper = w_middle.shape[1]
    panels = lax.axis_size("blk")
    groups = lax.axis_size("grp")
    me = lax.axis_index("blk")
    core, x, y = me & 1, (me >> 1) & 3, me >> 3

    def blk(value, partner):
        return lax.ppermute(value, "blk", [(i, partner(i)) for i in range(panels)])

    def on_core(value):
        return blk(value, lambda i: i ^ 1)

    def on_outer(value):
        return blk(value, lambda i: (i - 1 if i % 2 == 0 else i + 1) % panels)

    def on_x(value, d):
        return blk(value, lambda i: i // 8 * 8 + (i // 2 % 4 + d) % 4 * 2 + i % 2)

    def on_y(value, d):
        return blk(value, lambda i: (i // 8 + d) % 4 * 8 + i % 8)

    def on_z(value, d):
        return lax.ppermute(value, "grp", [(i, (i + d) % groups) for i in range(groups)])

    sums = send_targets(block_list[0], block_counts, pair_targets[0], panels).reshape(panels, 24, ROWS * PANEL)
    targets = lax.all_to_all(sums, "blk", 0, 0, tiled=True)
    targets = targets.reshape(24 * panels, ROWS * PANEL)

    right = jnp.dot(emb, w_right, preferred_element_type=F32).astype(BF)
    ids = cluster_ids[0].astype(BF)
    ids_row = jnp.pad(ids[None, :], ((0, 15), (0, hidden - PANEL)))
    right_own = jnp.concatenate([right, ids_row], axis=0)
    right_outer = on_outer(right_own)
    right_partner = on_core(right_own)

    left = jnp.dot(emb, w_left, preferred_element_type=F32).astype(BF)
    col_ids = jnp.stack([right_outer[PANEL, :PANEL], ids, right_partner[PANEL, :PANEL]])

    emb_pair = jnp.concatenate([emb, on_core(emb)], axis=0)
    embs = [emb_pair]
    for d in ORDER[1:]:
        embs.append(on_x(emb_pair, d))

    lg, r_outer, r_own, keep, sent = pair_grads(
        core[None],
        col_ids.astype(jnp.int32),
        jnp.pad(col_ids.astype(F32), ((0, 5), (0, 0))),
        left,
        right_outer,
        right_own,
        right_partner,
        targets,
        hidden_bias[None, :],
        w_middle.T,
        w_final[:, None],
    )

    first = core == 0
    got = on_core(sent)
    outer = on_outer(r_outer).astype(F32)
    over = lax.ppermute(r_outer, "blk", [(i, (i + 2) % panels) for i in range(1, panels, 2)]).astype(F32)
    r_partner = sent[PANEL : 2 * PANEL].astype(F32)
    rg = (r_own.astype(F32) + got[PANEL : 2 * PANEL].astype(F32) + outer).astype(BF)
    pair_right = (got[:PANEL].astype(F32) + r_partner + over).astype(BF)
    extra = keep.astype(F32) + got[2 * PANEL :].astype(F32)
    both = jnp.concatenate(
        [jnp.where(first, lg, rg), jnp.where(first, got[:PANEL], pair_right), extra.astype(BF)], axis=0
    )
    grad_local = jnp.dot(lg, w_left.T, preferred_element_type=F32) + jnp.dot(
        rg, w_right.T, preferred_element_type=F32
    )

    def column(d):
        return lax.dynamic_slice_in_dim(both, ((x + d) & 3) * 128, 128, 1)

    parts = [column(0)] + [on_x(column(d), d) for d in ORDER[1:]]
    total = weight_slice(embs, parts)
    piece = total.shape[0] // 4

    def rows(d):
        return lax.dynamic_slice_in_dim(total, ((y + d) & 3) * piece, piece, 0)

    parts = [rows(0)] + [on_y(rows(d), d) for d in ORDER[1:]]
    total = sum(p.astype(F32) for p in parts).astype(BF)
    total = (
        total.astype(F32)
        + lax.ppermute(total, "grp", [(i, i ^ 1) for i in range(groups)]).astype(F32)
    ).astype(BF)
    total = sum(p.astype(F32) for p in [total] + [on_z(total, d) for d in (2, 6, 4)]).astype(BF)
    total, grad_local = lax.optimization_barrier((total, grad_local))

    total = jnp.concatenate([total] + [on_y(total, d) for d in ORDER[1:]], axis=0)
    mine = [total] + [on_x(total, d) for d in ORDER[1:]]
    theirs = [on_core(p) for p in mine]
    devices = panels * groups
    scale = 1.0 / math.sqrt(devices * B_DEV * PANEL)
    vmem = pl.BlockSpec(memory_space=pltpu.VMEM)
    block = depth // 4
    grad_left, grad_right, grad_middle, grad_bias, grad_final = pl.pallas_call(
        lambda *refs: finish_kernel(scale, *refs),
        grid=(4,),
        out_shape=(
            jax.ShapeDtypeStruct((depth, hidden), F32),
            jax.ShapeDtypeStruct((depth, hidden), F32),
            jax.ShapeDtypeStruct((hidden, upper), F32),
            jax.ShapeDtypeStruct((1, hidden), F32),
            jax.ShapeDtypeStruct((1, upper), F32),
        ),
        in_specs=[pl.BlockSpec(memory_space=pltpu.SMEM)] + [vmem] * 8,
        out_specs=(
            pl.BlockSpec((block, hidden), lambda i: (i, 0)),
            pl.BlockSpec((block, hidden), lambda i: (i, 0)),
            pl.BlockSpec((hidden, upper), lambda i: (0, 0)),
            pl.BlockSpec((1, hidden), lambda i: (0, 0)),
            pl.BlockSpec((1, upper), lambda i: (0, 0)),
        ),
        scratch_shapes=[pltpu.VMEM((2, 4, 4 * piece, 128), BF)],
        compiler_params=pltpu.CompilerParams(vmem_limit_bytes=16 << 20),
        name="finish",
    )(jnp.stack([core, x, y]), *mine, *theirs)
    return (grad_local[None], grad_left, grad_right, grad_bias[0], grad_middle, grad_final[0])


def solution(mesh):
    return jax.shard_map(
        local,
        mesh=mesh,
        in_specs=(
            P("grp", "blk", None),
            P("grp", "blk"),
            P("grp", "blk", None),
            P("grp", "blk"),
            P("grp", "blk", None),
            P(),
            P(),
            P(),
            P(),
            P(),
        ),
        out_specs=(P("grp", "blk", None), P(), P(), P(), P(), P()),
        check_vma=False,
    )
```

```python
import math

import jax
import jax.numpy as jnp
from jax import lax
from jax.experimental import pallas as pl
from jax.experimental.pallas import tpu as pltpu
from jax.sharding import PartitionSpec as P

PANEL = 64
B_DEV = 8
ROWS = 8
CHUNK = 256
BF = jnp.bfloat16
F32 = jnp.float32


def forward(tile_at, left_s, right_s, hid_s, slope_s, rows=range(ROWS)):
    k = tile_at // 8
    left8 = left_s[pl.ds(pl.multiple_of(tile_at % 8 * ROWS, ROWS), ROWS), :]
    right = right_s[pl.ds(pl.multiple_of(k * PANEL, PANEL), PANEL), :]
    for a in rows:
        part = slice(a * PANEL, (a + 1) * PANEL)
        u = right.astype(BF) + jnp.broadcast_to(left8[a : a + 1, :], right.shape).astype(BF)
        p = jnp.tanh(u) + BF(1.0)
        h = u * p
        hid_s[part, :] = h
        slope_s[part, :] = p + h * (BF(2.0) - p)


def backward(
    tile_at, hid_s, slope_s, info_s, half_s, wmt_ref, wf_ref, lacc, racc, mid_acc, fin_acc
):
    col0 = pl.multiple_of(tile_at // 8 * PANEL, PANEL)
    row0 = pl.multiple_of(tile_at % 8 * ROWS, ROWS)
    wf = wf_ref[...]
    parts = [slice(c * CHUNK, (c + 1) * CHUNK) for c in range(ROWS * PANEL // CHUNK)]
    pre = [
        jnp.dot(hid_s[part, :], half_s[...], preferred_element_type=F32).T
        for part in parts
    ]
    terms, hiddens, fins = [], [], []
    for part, u in zip(parts, pre):
        p = jnp.tanh(u) + 1.0
        act = u * p
        predicted = jnp.sum(act * wf, axis=0, keepdims=True)
        pair_slope = info_s[tile_at, 1:2, part] * (
            info_s[tile_at, 2:3, part] * predicted - info_s[tile_at, 0:1, part]
        )
        grad_second = ((0.5 * pair_slope) * wf * (p + act * (2.0 - p))).astype(BF)
        fin = act * pair_slope
        fins.append(sum(fin[:, j * 128 : (j + 1) * 128] for j in range(CHUNK // 128)))
        hiddens.append(
            lax.dot_general(grad_second, wmt_ref[...], (((0,), (0,)), ((), ())), preferred_element_type=F32)
        )
        terms.append(jnp.dot(grad_second, hid_s[part, :], preferred_element_type=F32))
    fin_acc[...] += sum(fins)
    cols, rows = None, []
    for part, grad_hidden in zip(parts, hiddens):
        for a in range(CHUNK // PANEL):
            at = slice(part.start + a * PANEL, part.start + (a + 1) * PANEL)
            g = grad_hidden[a * PANEL : (a + 1) * PANEL, :] * slope_s[at, :].astype(F32)
            rows.append(jnp.sum(g, axis=0, keepdims=True))
            cols = g if cols is None else cols + g
    mid_acc[...] += sum(terms)
    racc[pl.ds(col0, PANEL), :] += cols
    lacc[pl.ds(row0, ROWS), :] += jnp.concatenate(rows, axis=0)


def pair_kernel(
    core,
    ids_s,
    ids_ref,
    left_ref,
    right_o,
    right_m,
    right_p,
    targets_ref,
    bias_ref,
    wmt_ref,
    wf_ref,
    out_left,
    out_outer,
    out_own,
    out_keep,
    out_sent,
    todo,
    panels_s,
    sems,
    left_s,
    right_s,
    info_s,
    half_s,
    hid_s,
    slope_s,
    lacc,
    racc,
    mid_acc,
    fin_acc,
):
    hidden = left_ref.shape[1]
    tile = ROWS * PANEL
    loads = [
        pltpu.make_async_copy(ref.at[0:PANEL, :], panels_s.at[n], sems.at[m])
        for m, (n, ref) in enumerate(
            ((0, left_ref), (1 + 2 * core[0], right_o), (2, right_m), (3 - 2 * core[0], right_p))
        )
    ]
    for copy in loads:
        copy.start()
    iota = lambda shape, axis: lax.broadcasted_iota(jnp.int32, shape, axis)
    begin = jnp.sum(jnp.where((ids_ref[...] < ids_s[1, PANEL // 2].astype(F32)) & (iota((8, PANEL), 0) < 3), 1, 0))
    shift = PANEL - (begin & (PANEL - 1))

    def scan(i, n):
        j, rt = i // 8, i % 8
        start = jnp.maximum(j * PANEL - shift, 0)
        end = jnp.minimum(j * PANEL - shift + PANEL - 1, 3 * PANEL - 1)
        last = jnp.maximum(end, 0)
        meets = (
            (end >= 0)
            & (ids_s[1, rt * ROWS] <= ids_s[last // PANEL, last % PANEL])
            & (ids_s[start // PANEL, start % PANEL] <= ids_s[1, rt * ROWS + ROWS - 1])
        )
        todo[n] = i
        return n + meets.astype(jnp.int32)

    n_todo = lax.fori_loop(0, 32, scan, 0)
    half_s[...] = (wmt_ref[...].astype(F32) * 0.5).T.astype(BF)
    n_src = targets_ref.shape[0]
    tsum = jnp.dot(
        (iota((24, n_src), 1) % 24 == iota((24, n_src), 0)).astype(BF), targets_ref[...], preferred_element_type=F32
    )
    ids = ids_ref[...]
    spread = (iota((PANEL, tile), 0) % ROWS == iota((PANEL, tile), 1) // PANEL).astype(BF)
    repeat = (iota((PANEL, tile), 0) == iota((PANEL, tile), 1) % PANEL).astype(BF)
    row_ids = jnp.where(iota((8, PANEL), 1) // ROWS == iota((8, PANEL), 0), ids[1:2, :], 0.0)
    row_ids = jnp.dot(row_ids.astype(BF), spread, preferred_element_type=F32)
    col_ids = jnp.dot(ids.astype(BF), repeat, preferred_element_type=F32)
    lane = iota((8, tile), 1)
    itself = iota((8, tile), 0) * ROWS + lane // PANEL == lane % PANEL
    infos = []
    for k in range(3):
        same = row_ids == col_ids[k : k + 1, :]
        mask = jnp.where(same & ~itself if k == 1 else same, 16.0, 0.0)
        count = jnp.max(
            jnp.where(iota((1, tile), 1) == k * (PANEL + 1), tsum[8:9, :], 0.0), axis=1, keepdims=True
        )
        infos.append((tsum[k * 8 : k * 8 + 8, :], mask, jnp.broadcast_to(count, (8, tile))))
    ahead, behind = lax.rem(shift, tile), lax.rem(shift + tile - PANEL, tile)
    for j in range(4):
        for n in range(3):
            here = pltpu.roll(infos[j][n], ahead, 1) if j < 3 else jnp.zeros((8, tile), F32)
            before = pltpu.roll(infos[j - 1][n], behind, 1) if j > 0 else jnp.zeros((8, tile), F32)
            moved = jnp.where(lane % PANEL >= shift, here, before)
            for rt in range(8):
                info_s[j * 8 + rt, n : n + 1, :] = moved[rt : rt + 1, :]
    lacc[...] = jnp.zeros_like(lacc)
    racc[...] = jnp.zeros_like(racc)
    mid_acc[...] = jnp.zeros_like(mid_acc)
    fin_acc[...] = jnp.zeros_like(fin_acc)
    for copy in loads:
        copy.wait()
    left_s[...] = (panels_s[0].astype(F32) + bias_ref[...]) * 0.5
    place = (iota((4 * PANEL, 3 * PANEL), 0) == iota((4 * PANEL, 3 * PANEL), 1) + shift).astype(BF)
    rights = jnp.concatenate([panels_s[k + 1] for k in range(3)], axis=0)
    right_s[...] = jnp.dot(place, rights, preferred_element_type=F32) * 0.5
    rest = (info_s, half_s, wmt_ref, wf_ref, lacc, racc, mid_acc, fin_acc)

    def step(i, carry):
        forward(todo[i], left_s, right_s, hid_s, slope_s)
        backward(todo[i], hid_s, slope_s, *rest)
        return carry

    lax.fori_loop(0, n_todo, step, 0)
    left = lacc[...] * 0.5
    out_left[...] = left.astype(BF)
    back = (iota((3 * PANEL, 4 * PANEL), 1) == iota((3 * PANEL, 4 * PANEL), 0) + shift).astype(BF)
    total = racc[...] * 0.5
    high = total.astype(BF)
    low = (total - high.astype(F32)).astype(BF)
    right_s[0 : 3 * PANEL, :] = jnp.dot(back, high, preferred_element_type=F32) + jnp.dot(
        back, low, preferred_element_type=F32
    )
    at = pl.multiple_of(2 * PANEL * core[0], PANEL)
    outer = right_s[pl.ds(at, PANEL), :].astype(BF)
    own = right_s[PANEL : 2 * PANEL, :].astype(BF)
    partner = right_s[pl.ds(pl.multiple_of(2 * PANEL - at, PANEL), PANEL), :].astype(BF)
    out_outer[...] = outer
    out_own[...] = own
    out_sent[PANEL : 2 * PANEL, :] = partner

    def middle(ref, start):
        for j in range(hidden // 128):
            block = slice(j * 128, (j + 1) * 128)
            ref[start : start + 128, block] = mid_acc[:, block].T.astype(BF)

    def small(ref, start):
        ref[start : start + 128, :] = jnp.zeros((128, hidden), BF)
        ref[start : start + 1, :] = jnp.sum(left, axis=0, keepdims=True).astype(BF)
        ref[start + 16 : start + 17, 0:128] = jnp.sum(fin_acc[...].T, axis=0, keepdims=True).astype(BF)

    @pl.when(core[0] == 0)
    def _():
        out_sent[0:PANEL, :] = own
        small(out_sent, 2 * PANEL)
        middle(out_keep, 0)

    @pl.when(core[0] != 0)
    def _():
        out_sent[0:PANEL, :] = left.astype(BF)
        middle(out_sent, 2 * PANEL)
        small(out_keep, 0)


def pair_grads(core, ids_s, ids, left, right_o, right_m, right_p, targets, bias, wmt, wf):
    hidden = left.shape[1]
    upper = wmt.shape[0]
    tile = ROWS * PANEL
    vmem = pl.BlockSpec(memory_space=pltpu.VMEM)
    panel = jax.ShapeDtypeStruct((PANEL, hidden), BF)
    return pl.pallas_call(
        pair_kernel,
        out_shape=(
            panel,
            panel,
            panel,
            jax.ShapeDtypeStruct((upper, hidden), BF),
            jax.ShapeDtypeStruct((2 * PANEL + upper, hidden), BF),
        ),
        in_specs=[pl.BlockSpec(memory_space=pltpu.SMEM)] * 2
        + [vmem]
        + [pl.BlockSpec(memory_space=pltpu.HBM)] * 4
        + [vmem] * 4,
        out_specs=(vmem,) * 5,
        scratch_shapes=[
            pltpu.SMEM((40,), jnp.int32),
            pltpu.VMEM((4, PANEL, hidden), BF),
            pltpu.SemaphoreType.DMA((4,)),
            pltpu.VMEM((PANEL, hidden), F32),
            pltpu.VMEM((4 * PANEL, hidden), F32),
            pltpu.VMEM((32, 8, tile), F32),
            pltpu.VMEM((hidden, upper), BF),
            pltpu.VMEM((tile, hidden), BF),
            pltpu.VMEM((tile, hidden), BF),
            pltpu.VMEM((PANEL, hidden), F32),
            pltpu.VMEM((4 * PANEL, hidden), F32),
            pltpu.VMEM((upper, hidden), F32),
            pltpu.VMEM((upper, 128), F32),
        ],
        compiler_params=pltpu.CompilerParams(vmem_limit_bytes=24 << 20),
        cost_estimate=pl.CostEstimate(
            flops=10 * 24 * tile * hidden * upper, bytes_accessed=2 << 20, transcendentals=24 * tile * hidden
        ),
        name="pair_grads",
    )(core, ids_s, ids, *[pltpu.with_memory_space_constraint(v, pltpu.HBM) for v in (left, right_o, right_m, right_p)], targets, bias, wmt, wf)


def send_kernel(blocks, live, targets_ref, out_ref, acc):
    tile = out_ref.shape[1]
    acc[...] = jnp.zeros_like(acc)
    lane = lax.broadcasted_iota(jnp.int32, (1, tile), 1)
    counters = (lane == 0) | (lane == PANEL + 1) | (lane == 2 * (PANEL + 1))

    def slot(i, carry):
        row = blocks[0, i]
        side = blocks[1, i] - row + 1
        to = row * 3 + side
        for rt in range(8):
            value = targets_ref[pl.ds(i, 1), rt * tile : (rt + 1) * tile]
            if rt == 0:
                value = jnp.where(counters & (side == 1), 0.0, value)
            acc[to, rt : rt + 1, :] += value
        acc[row * 3 + 1, 0:1, :] += jnp.where(lane == side * (PANEL + 1), 1.0, 0.0)
        return carry

    lax.fori_loop(0, live[0, 0], slot, 0)
    for p in range(acc.shape[0]):
        out_ref[p * 8 : (p + 1) * 8, :] = acc[p].astype(BF)


def send_targets(blocks, live, targets, panels):
    tile = ROWS * PANEL
    smem = pl.BlockSpec(memory_space=pltpu.SMEM)
    vmem = pl.BlockSpec(memory_space=pltpu.VMEM)
    return pl.pallas_call(
        send_kernel,
        out_shape=jax.ShapeDtypeStruct((24 * panels, tile), BF),
        in_specs=[smem, smem, vmem],
        out_specs=vmem,
        scratch_shapes=[pltpu.VMEM((3 * panels, 8, tile), F32)],
        compiler_params=pltpu.CompilerParams(vmem_limit_bytes=8 << 20),
        name="send_targets",
    )(blocks, live, targets)


def slice_kernel(*refs):
    embs, parts, out = refs[:4], refs[4:8], refs[8]
    depth = embs[0].shape[1]
    rows = embs[0].shape[0]
    total = extra = None
    for emb, part in zip(embs, parts):
        term = lax.dot_general(
            emb[...], part[0:rows, :], (((0,), (0,)), ((), ())), preferred_element_type=F32
        )
        more = part[rows:, :].astype(F32)
        total = term if total is None else total + term
        extra = more if extra is None else extra + more
    out[0:depth, :] = total.astype(BF)
    out[depth:, :] = extra.astype(BF)


def weight_slice(embs, parts):
    rows, depth = embs[0].shape
    vmem = pl.BlockSpec(memory_space=pltpu.VMEM)
    return pl.pallas_call(
        slice_kernel,
        out_shape=jax.ShapeDtypeStruct((depth + parts[0].shape[0] - rows, parts[0].shape[1]), BF),
        in_specs=[vmem] * 8,
        out_specs=vmem,
        compiler_params=pltpu.CompilerParams(vmem_limit_bytes=16 << 20),
        name="weight_slice",
    )(*embs, *parts)


ORDER = (0, 1, 3, 2)


def finish_kernel(scale, pos, *refs):
    pieces, (left_ref, right_ref, mid_ref, bias_ref, fin_ref, whole) = refs[:8], refs[8:]
    part = whole.shape[2] // 4
    depth = whole.shape[2] - 128
    block = left_ref.shape[0]

    @pl.when(pl.program_id(0) == 0)
    def _():
        for n, ref in enumerate(pieces):
            side = pos[0] if n < 4 else 1 - pos[0]
            column = lax.rem(pos[1] - ORDER[n % 4] + 4, 4)
            for m, dy in enumerate(ORDER):
                row = pl.multiple_of(lax.rem(pos[2] - dy + 4, 4) * part, 32)
                whole[side, column, pl.ds(row, part), :] = ref[m * part : (m + 1) * part, :]
        for j in range(4):
            lanes = slice(j * 128, (j + 1) * 128)
            mid_ref[lanes, :] = whole[0, j, depth : depth + 128, :].astype(F32) * scale
            bias_ref[:, lanes] = whole[1, j, depth : depth + 1, :].astype(F32) * scale
        fin_ref[...] = whole[1, 0, depth + 16 : depth + 17, :].astype(F32) * scale

    rows = pl.ds(pl.multiple_of(pl.program_id(0) * block, block), block)
    for j in range(4):
        lanes = slice(j * 128, (j + 1) * 128)
        left_ref[:, lanes] = whole[0, j, rows, :].astype(F32) * scale
        right_ref[:, lanes] = whole[1, j, rows, :].astype(F32) * scale


def local(
    embeddings,
    cluster_ids,
    block_list,
    block_counts,
    pair_targets,
    w_left,
    w_right,
    hidden_bias,
    w_middle,
    w_final,
):
    emb = embeddings[0]
    depth = emb.shape[1]
    hidden = w_left.shape[1]
    upper = w_middle.shape[1]
    panels = lax.axis_size("blk")
    groups = lax.axis_size("grp")
    me = lax.axis_index("blk")
    core, x, y = me & 1, (me >> 1) & 3, me >> 3

    def blk(value, partner):
        return lax.ppermute(value, "blk", [(i, partner(i)) for i in range(panels)])

    def on_core(value):
        return blk(value, lambda i: i ^ 1)

    def on_outer(value):
        return blk(value, lambda i: (i - 1 if i % 2 == 0 else i + 1) % panels)

    def on_x(value, d):
        return blk(value, lambda i: i // 8 * 8 + (i // 2 % 4 + d) % 4 * 2 + i % 2)

    def on_y(value, d):
        return blk(value, lambda i: (i // 8 + d) % 4 * 8 + i % 8)

    def on_z(value, d):
        return lax.ppermute(value, "grp", [(i, (i + d) % groups) for i in range(groups)])

    sums = send_targets(block_list[0].T, block_counts, pair_targets[0], panels).reshape(panels, 24, ROWS * PANEL)
    targets = lax.all_to_all(sums, "blk", 0, 0, tiled=True)
    targets = targets.reshape(24 * panels, ROWS * PANEL)

    right = jnp.dot(emb, w_right, preferred_element_type=F32).astype(BF)
    ids = cluster_ids[0].astype(BF)
    ids_row = jnp.pad(ids[None, :], ((0, 15), (0, hidden - PANEL)))
    right_own = jnp.concatenate([right, ids_row], axis=0)
    right_outer = on_outer(right_own)
    right_partner = on_core(right_own)

    left = jnp.dot(emb, w_left, preferred_element_type=F32).astype(BF)
    outer_ids = right_outer[PANEL, :PANEL]
    partner_ids = right_partner[PANEL, :PANEL]
    before = jnp.where(me == 0, BF(-1), jnp.where(core == 0, outer_ids, partner_ids))
    after = jnp.where(me == panels - 1, BF(127), jnp.where(core == 0, partner_ids, outer_ids))
    col_ids = jnp.stack([before, ids, after])

    emb_pair = jnp.concatenate([emb, on_core(emb)], axis=0)
    embs = [emb_pair]
    for d in ORDER[1:]:
        embs.append(on_x(emb_pair, d))

    lg, r_outer, r_own, keep, sent = pair_grads(
        core[None],
        col_ids.astype(jnp.int32),
        jnp.pad(col_ids.astype(F32), ((0, 5), (0, 0))),
        left,
        right_outer,
        right_own,
        right_partner,
        targets,
        hidden_bias[None, :],
        w_middle.T,
        w_final[:, None],
    )

    first = core == 0
    got = on_core(sent)
    outer = on_outer(r_outer).astype(F32)
    over = lax.ppermute(r_outer, "blk", [(i, (i + 2) % panels) for i in range(1, panels, 2)]).astype(F32)
    r_partner = sent[PANEL : 2 * PANEL].astype(F32)
    rg = (r_own.astype(F32) + got[PANEL : 2 * PANEL].astype(F32) + outer).astype(BF)
    pair_right = (got[:PANEL].astype(F32) + r_partner + over).astype(BF)
    extra = keep.astype(F32) + got[2 * PANEL :].astype(F32)
    both = jnp.concatenate(
        [jnp.where(first, lg, rg), jnp.where(first, got[:PANEL], pair_right), extra.astype(BF)], axis=0
    )
    grad_local = jnp.dot(lg, w_left.T, preferred_element_type=F32) + jnp.dot(
        rg, w_right.T, preferred_element_type=F32
    )

    def column(d):
        return lax.dynamic_slice_in_dim(both, ((x + d) & 3) * 128, 128, 1)

    parts = [column(0)] + [on_x(column(d), d) for d in ORDER[1:]]
    total = weight_slice(embs, parts)
    piece = total.shape[0] // 4

    def rows(d):
        return lax.dynamic_slice_in_dim(total, ((y + d) & 3) * piece, piece, 0)

    parts = [rows(0)] + [on_y(rows(d), d) for d in ORDER[1:]]
    total = sum(p.astype(F32) for p in parts).astype(BF)
    total = (
        total.astype(F32)
        + lax.ppermute(total, "grp", [(i, i ^ 1) for i in range(groups)]).astype(F32)
    ).astype(BF)
    total = sum(p.astype(F32) for p in [total] + [on_z(total, d) for d in (2, 6, 4)]).astype(BF)
    total, grad_local = lax.optimization_barrier((total, grad_local))

    total = jnp.concatenate([total] + [on_y(total, d) for d in ORDER[1:]], axis=0)
    mine = [total] + [on_x(total, d) for d in ORDER[1:]]
    theirs = [on_core(p) for p in mine]
    devices = panels * groups
    scale = 1.0 / math.sqrt(devices * B_DEV * PANEL)
    vmem = pl.BlockSpec(memory_space=pltpu.VMEM)
    block = depth // 4
    grad_left, grad_right, grad_middle, grad_bias, grad_final = pl.pallas_call(
        lambda *refs: finish_kernel(scale, *refs),
        grid=(4,),
        out_shape=(
            jax.ShapeDtypeStruct((depth, hidden), F32),
            jax.ShapeDtypeStruct((depth, hidden), F32),
            jax.ShapeDtypeStruct((hidden, upper), F32),
            jax.ShapeDtypeStruct((1, hidden), F32),
            jax.ShapeDtypeStruct((1, upper), F32),
        ),
        in_specs=[pl.BlockSpec(memory_space=pltpu.SMEM)] + [vmem] * 8,
        out_specs=(
            pl.BlockSpec((block, hidden), lambda i: (i, 0)),
            pl.BlockSpec((block, hidden), lambda i: (i, 0)),
            pl.BlockSpec((hidden, upper), lambda i: (0, 0)),
            pl.BlockSpec((1, hidden), lambda i: (0, 0)),
            pl.BlockSpec((1, upper), lambda i: (0, 0)),
        ),
        scratch_shapes=[pltpu.VMEM((2, 4, 4 * piece, 128), BF)],
        compiler_params=pltpu.CompilerParams(vmem_limit_bytes=16 << 20),
        name="finish",
    )(jnp.stack([core, x, y]), *mine, *theirs)
    return (grad_local[None], grad_left, grad_right, grad_bias[0], grad_middle, grad_final[0])


def solution(mesh):
    return jax.shard_map(
        local,
        mesh=mesh,
        in_specs=(
            P("grp", "blk", None),
            P("grp", "blk"),
            P("grp", "blk", None),
            P("grp", "blk"),
            P("grp", "blk", None),
            P(),
            P(),
            P(),
            P(),
            P(),
        ),
        out_specs=(P("grp", "blk", None), P(), P(), P(), P(), P()),
        check_vma=False,
    )
```

```python
import math

import jax
import jax.numpy as jnp
from jax import lax
from jax.experimental import pallas as pl
from jax.experimental.pallas import tpu as pltpu
from jax.sharding import PartitionSpec as P

PANEL = 64
B_DEV = 8
ROWS = 8
CHUNK = 256
BF = jnp.bfloat16
F32 = jnp.float32


def forward(tile_at, left_s, right_s, hid_s, slope_s, rows=range(ROWS)):
    k = tile_at // 8
    left8 = left_s[pl.ds(pl.multiple_of(tile_at % 8 * ROWS, ROWS), ROWS), :]
    right = right_s[pl.ds(pl.multiple_of(k * PANEL, PANEL), PANEL), :]
    for a in rows:
        part = slice(a * PANEL, (a + 1) * PANEL)
        u = right.astype(BF) + jnp.broadcast_to(left8[a : a + 1, :], right.shape).astype(BF)
        p = jnp.tanh(u) + BF(1.0)
        h = u * p
        hid_s[part, :] = h
        slope_s[part, :] = p + h * (BF(2.0) - p)


def backward(
    tile_at, hid_s, slope_s, info_s, half_s, wmt_ref, wf_ref, lacc, racc, mid_acc, fin_acc
):
    col0 = pl.multiple_of(tile_at // 8 * PANEL, PANEL)
    row0 = pl.multiple_of(tile_at % 8 * ROWS, ROWS)
    wf = wf_ref[...]
    parts = [slice(c * CHUNK, (c + 1) * CHUNK) for c in range(ROWS * PANEL // CHUNK)]
    pre = [
        jnp.dot(hid_s[part, :], half_s[...], preferred_element_type=F32).T
        for part in parts
    ]
    terms, hiddens, fins = [], [], []
    for part, u in zip(parts, pre):
        p = jnp.tanh(u) + 1.0
        act = u * p
        predicted = jnp.sum(act * wf, axis=0, keepdims=True)
        pair_slope = info_s[tile_at, 1:2, part] * (
            info_s[tile_at, 2:3, part] * predicted - info_s[tile_at, 0:1, part]
        )
        grad_second = ((0.5 * pair_slope) * wf * (p + act * (2.0 - p))).astype(BF)
        fin = act * pair_slope
        fins.append(sum(fin[:, j * 128 : (j + 1) * 128] for j in range(CHUNK // 128)))
        hiddens.append(
            lax.dot_general(grad_second, wmt_ref[...], (((0,), (0,)), ((), ())), preferred_element_type=F32)
        )
        terms.append(jnp.dot(grad_second, hid_s[part, :], preferred_element_type=F32))
    fin_acc[...] += sum(fins)
    cols, rows = None, []
    for part, grad_hidden in zip(parts, hiddens):
        for a in range(CHUNK // PANEL):
            at = slice(part.start + a * PANEL, part.start + (a + 1) * PANEL)
            g = grad_hidden[a * PANEL : (a + 1) * PANEL, :] * slope_s[at, :].astype(F32)
            rows.append(jnp.sum(g, axis=0, keepdims=True))
            cols = g if cols is None else cols + g
    mid_acc[...] += sum(terms)
    racc[pl.ds(col0, PANEL), :] += cols
    lacc[pl.ds(row0, ROWS), :] += jnp.concatenate(rows, axis=0)


def pair_kernel(
    core,
    ids_s,
    ids_ref,
    left_ref,
    right_o,
    right_m,
    right_p,
    targets_ref,
    bias_ref,
    wmt_ref,
    wf_ref,
    out_left,
    out_outer,
    out_own,
    out_keep,
    out_sent,
    todo,
    panels_s,
    sems,
    left_s,
    right_s,
    info_s,
    half_s,
    hid_s,
    slope_s,
    lacc,
    racc,
    mid_acc,
    fin_acc,
):
    hidden = left_ref.shape[1]
    tile = ROWS * PANEL
    loads = [
        pltpu.make_async_copy(ref.at[0:PANEL, :], panels_s.at[n], sems.at[m])
        for m, (n, ref) in enumerate(
            ((0, left_ref), (1 + 2 * core[0], right_o), (2, right_m), (3 - 2 * core[0], right_p))
        )
    ]
    for copy in loads:
        copy.start()
    iota = lambda shape, axis: lax.broadcasted_iota(jnp.int32, shape, axis)
    begin = jnp.sum(jnp.where((ids_ref[...] < ids_s[1, PANEL // 2].astype(F32)) & (iota((8, PANEL), 0) < 3), 1, 0))
    shift = PANEL - (begin & (PANEL - 1))

    def scan(i, n):
        j, rt = i // 8, i % 8
        start = jnp.maximum(j * PANEL - shift, 0)
        end = jnp.minimum(j * PANEL - shift + PANEL - 1, 3 * PANEL - 1)
        last = jnp.maximum(end, 0)
        meets = (
            (end >= 0)
            & (ids_s[1, rt * ROWS] <= ids_s[last // PANEL, last % PANEL])
            & (ids_s[start // PANEL, start % PANEL] <= ids_s[1, rt * ROWS + ROWS - 1])
        )
        todo[n] = i
        return n + meets.astype(jnp.int32)

    n_todo = lax.fori_loop(0, 32, scan, 0)
    half_s[...] = (wmt_ref[...].astype(F32) * 0.5).T.astype(BF)
    n_src = targets_ref.shape[0]
    tsum = jnp.dot(
        (iota((24, n_src), 1) % 24 == iota((24, n_src), 0)).astype(BF), targets_ref[...], preferred_element_type=F32
    )
    ids = ids_ref[...]
    spread = (iota((PANEL, tile), 0) % ROWS == iota((PANEL, tile), 1) // PANEL).astype(BF)
    repeat = (iota((PANEL, tile), 0) == iota((PANEL, tile), 1) % PANEL).astype(BF)
    row_ids = jnp.where(iota((8, PANEL), 1) // ROWS == iota((8, PANEL), 0), ids[1:2, :], 0.0)
    row_ids = jnp.dot(row_ids.astype(BF), spread, preferred_element_type=F32)
    col_ids = jnp.dot(ids.astype(BF), repeat, preferred_element_type=F32)
    lane = iota((8, tile), 1)
    itself = iota((8, tile), 0) * ROWS + lane // PANEL == lane % PANEL
    infos = []
    for k in range(3):
        same = row_ids == col_ids[k : k + 1, :]
        mask = jnp.where(same & ~itself if k == 1 else same, 16.0, 0.0)
        count = jnp.max(
            jnp.where(iota((1, tile), 1) == k * (PANEL + 1), tsum[8:9, :], 0.0), axis=1, keepdims=True
        )
        infos.append((tsum[k * 8 : k * 8 + 8, :], mask, jnp.broadcast_to(count, (8, tile))))
    ahead, behind = lax.rem(shift, tile), lax.rem(shift + tile - PANEL, tile)
    for j in range(4):
        for n in range(3):
            here = pltpu.roll(infos[j][n], ahead, 1) if j < 3 else jnp.zeros((8, tile), F32)
            before = pltpu.roll(infos[j - 1][n], behind, 1) if j > 0 else jnp.zeros((8, tile), F32)
            moved = jnp.where(lane % PANEL >= shift, here, before)
            for rt in range(8):
                info_s[j * 8 + rt, n : n + 1, :] = moved[rt : rt + 1, :]
    lacc[...] = jnp.zeros_like(lacc)
    racc[...] = jnp.zeros_like(racc)
    mid_acc[...] = jnp.zeros_like(mid_acc)
    fin_acc[...] = jnp.zeros_like(fin_acc)
    for copy in loads:
        copy.wait()
    left_s[...] = (panels_s[0].astype(F32) + bias_ref[...]) * 0.5
    place = (iota((4 * PANEL, 3 * PANEL), 0) == iota((4 * PANEL, 3 * PANEL), 1) + shift).astype(BF)
    rights = jnp.concatenate([panels_s[k + 1] for k in range(3)], axis=0)
    right_s[...] = jnp.dot(place, rights, preferred_element_type=F32) * 0.5
    rest = (info_s, half_s, wmt_ref, wf_ref, lacc, racc, mid_acc, fin_acc)

    def step(i, carry):
        forward(todo[i], left_s, right_s, hid_s, slope_s)
        backward(todo[i], hid_s, slope_s, *rest)
        return carry

    lax.fori_loop(0, n_todo, step, 0)
    left = lacc[...] * 0.5
    out_left[...] = left.astype(BF)
    back = (iota((3 * PANEL, 4 * PANEL), 1) == iota((3 * PANEL, 4 * PANEL), 0) + shift).astype(BF)
    total = racc[...] * 0.5
    high = total.astype(BF)
    low = (total - high.astype(F32)).astype(BF)
    right_s[0 : 3 * PANEL, :] = jnp.dot(back, high, preferred_element_type=F32) + jnp.dot(
        back, low, preferred_element_type=F32
    )
    at = pl.multiple_of(2 * PANEL * core[0], PANEL)
    outer = right_s[pl.ds(at, PANEL), :].astype(BF)
    own = right_s[PANEL : 2 * PANEL, :].astype(BF)
    partner = right_s[pl.ds(pl.multiple_of(2 * PANEL - at, PANEL), PANEL), :].astype(BF)
    out_outer[...] = outer
    out_own[...] = own
    out_sent[PANEL : 2 * PANEL, :] = partner

    def middle(ref, start):
        for j in range(hidden // 128):
            block = slice(j * 128, (j + 1) * 128)
            ref[start : start + 128, block] = mid_acc[:, block].T.astype(BF)

    def small(ref, start):
        ref[start : start + 128, :] = jnp.zeros((128, hidden), BF)
        ref[start : start + 1, :] = jnp.sum(left, axis=0, keepdims=True).astype(BF)
        ref[start + 16 : start + 17, 0:128] = jnp.sum(fin_acc[...].T, axis=0, keepdims=True).astype(BF)

    @pl.when(core[0] == 0)
    def _():
        out_sent[0:PANEL, :] = own
        small(out_sent, 2 * PANEL)
        middle(out_keep, 0)

    @pl.when(core[0] != 0)
    def _():
        out_sent[0:PANEL, :] = left.astype(BF)
        middle(out_sent, 2 * PANEL)
        small(out_keep, 0)


def pair_grads(core, ids_s, ids, left, right_o, right_m, right_p, targets, bias, wmt, wf):
    hidden = left.shape[1]
    upper = wmt.shape[0]
    tile = ROWS * PANEL
    vmem = pl.BlockSpec(memory_space=pltpu.VMEM)
    panel = jax.ShapeDtypeStruct((PANEL, hidden), BF)
    return pl.pallas_call(
        pair_kernel,
        out_shape=(
            panel,
            panel,
            panel,
            jax.ShapeDtypeStruct((upper, hidden), BF),
            jax.ShapeDtypeStruct((2 * PANEL + upper, hidden), BF),
        ),
        in_specs=[pl.BlockSpec(memory_space=pltpu.SMEM)] * 2
        + [vmem]
        + [pl.BlockSpec(memory_space=pltpu.HBM)] * 4
        + [vmem] * 4,
        out_specs=(vmem,) * 5,
        scratch_shapes=[
            pltpu.SMEM((40,), jnp.int32),
            pltpu.VMEM((4, PANEL, hidden), BF),
            pltpu.SemaphoreType.DMA((4,)),
            pltpu.VMEM((PANEL, hidden), F32),
            pltpu.VMEM((4 * PANEL, hidden), F32),
            pltpu.VMEM((32, 8, tile), F32),
            pltpu.VMEM((hidden, upper), BF),
            pltpu.VMEM((tile, hidden), BF),
            pltpu.VMEM((tile, hidden), BF),
            pltpu.VMEM((PANEL, hidden), F32),
            pltpu.VMEM((4 * PANEL, hidden), F32),
            pltpu.VMEM((upper, hidden), F32),
            pltpu.VMEM((upper, 128), F32),
        ],
        compiler_params=pltpu.CompilerParams(vmem_limit_bytes=24 << 20),
        cost_estimate=pl.CostEstimate(
            flops=10 * 24 * tile * hidden * upper, bytes_accessed=2 << 20, transcendentals=24 * tile * hidden
        ),
        name="pair_grads",
    )(core, ids_s, ids, *[pltpu.with_memory_space_constraint(v, pltpu.HBM) for v in (left, right_o, right_m, right_p)], targets, bias, wmt, wf)


def send_kernel(blocks, live, targets_ref, out_ref, acc):
    tile = out_ref.shape[1]
    acc[...] = jnp.zeros_like(acc)
    lane = lax.broadcasted_iota(jnp.int32, (1, tile), 1)
    counters = (lane == 0) | (lane == PANEL + 1) | (lane == 2 * (PANEL + 1))

    def slot(i, carry):
        row = blocks[0, i]
        side = blocks[1, i] - row + 1
        to = row * 3 + side
        for rt in range(8):
            value = targets_ref[pl.ds(i, 1), rt * tile : (rt + 1) * tile]
            if rt == 0:
                value = jnp.where(counters & (side == 1), 0.0, value)
            acc[to, rt : rt + 1, :] += value
        acc[row * 3 + 1, 0:1, :] += jnp.where(lane == side * (PANEL + 1), 1.0, 0.0)
        return carry

    lax.fori_loop(0, live[0, 0], slot, 0)
    for p in range(acc.shape[0]):
        out_ref[p * 8 : (p + 1) * 8, :] = acc[p].astype(BF)


def send_targets(blocks, live, targets, panels):
    tile = ROWS * PANEL
    smem = pl.BlockSpec(memory_space=pltpu.SMEM)
    vmem = pl.BlockSpec(memory_space=pltpu.VMEM)
    return pl.pallas_call(
        send_kernel,
        out_shape=jax.ShapeDtypeStruct((24 * panels, tile), BF),
        in_specs=[smem, smem, vmem],
        out_specs=vmem,
        scratch_shapes=[pltpu.VMEM((3 * panels, 8, tile), F32)],
        compiler_params=pltpu.CompilerParams(vmem_limit_bytes=8 << 20),
        name="send_targets",
    )(blocks, live, targets)


def slice_kernel(*refs):
    embs, parts, out, emb_s, part_s = refs[:8], refs[8:12], refs[12], refs[13], refs[14]
    rows, depth = embs[0].shape
    for n, ref in enumerate(embs):
        emb_s[n * rows : (n + 1) * rows, :] = ref[...]
    for n, ref in enumerate(parts):
        part_s[n * 2 * rows : (n + 1) * 2 * rows, :] = ref[0 : 2 * rows, :]
    out[0:depth, :] = lax.dot_general(
        emb_s[...], part_s[...], (((0,), (0,)), ((), ())), preferred_element_type=F32
    ).astype(BF)
    out[depth:, :] = sum(ref[2 * rows :, :].astype(F32) for ref in parts).astype(BF)


def weight_slice(embs, parts):
    rows, depth = embs[0].shape
    width = parts[0].shape[1]
    vmem = pl.BlockSpec(memory_space=pltpu.VMEM)
    return pl.pallas_call(
        slice_kernel,
        out_shape=jax.ShapeDtypeStruct((depth + parts[0].shape[0] - 2 * rows, width), BF),
        in_specs=[vmem] * 12,
        out_specs=vmem,
        scratch_shapes=[pltpu.VMEM((8 * rows, depth), BF), pltpu.VMEM((8 * rows, width), BF)],
        compiler_params=pltpu.CompilerParams(vmem_limit_bytes=16 << 20),
        name="weight_slice",
    )(*embs, *parts)


ORDER = (0, 1, 3, 2)


def finish_kernel(scale, pos, *refs):
    pieces, (left_ref, right_ref, mid_ref, bias_ref, fin_ref, whole) = refs[:8], refs[8:]
    part = whole.shape[2] // 4
    depth = whole.shape[2] - 128
    block = left_ref.shape[0]

    @pl.when(pl.program_id(0) == 0)
    def _():
        for n, ref in enumerate(pieces):
            side = pos[0] if n < 4 else 1 - pos[0]
            column = lax.rem(pos[1] - ORDER[n % 4] + 4, 4)
            for m, dy in enumerate(ORDER):
                row = pl.multiple_of(lax.rem(pos[2] - dy + 4, 4) * part, 32)
                whole[side, column, pl.ds(row, part), :] = ref[m * part : (m + 1) * part, :]
        for j in range(4):
            lanes = slice(j * 128, (j + 1) * 128)
            mid_ref[lanes, :] = whole[0, j, depth : depth + 128, :].astype(F32) * scale
            bias_ref[:, lanes] = whole[1, j, depth : depth + 1, :].astype(F32) * scale
        fin_ref[...] = whole[1, 0, depth + 16 : depth + 17, :].astype(F32) * scale

    rows = pl.ds(pl.multiple_of(pl.program_id(0) * block, block), block)
    for j in range(4):
        lanes = slice(j * 128, (j + 1) * 128)
        left_ref[:, lanes] = whole[0, j, rows, :].astype(F32) * scale
        right_ref[:, lanes] = whole[1, j, rows, :].astype(F32) * scale


def local(
    embeddings,
    cluster_ids,
    block_list,
    block_counts,
    pair_targets,
    w_left,
    w_right,
    hidden_bias,
    w_middle,
    w_final,
):
    emb = embeddings[0]
    depth = emb.shape[1]
    hidden = w_left.shape[1]
    upper = w_middle.shape[1]
    panels = lax.axis_size("blk")
    groups = lax.axis_size("grp")
    me = lax.axis_index("blk")
    core, x, y = me & 1, (me >> 1) & 3, me >> 3

    def blk(value, partner):
        return lax.ppermute(value, "blk", [(i, partner(i)) for i in range(panels)])

    def on_core(value):
        return blk(value, lambda i: i ^ 1)

    def on_outer(value):
        return blk(value, lambda i: (i - 1 if i % 2 == 0 else i + 1) % panels)

    def on_x(value, d):
        return blk(value, lambda i: i // 8 * 8 + (i // 2 % 4 + d) % 4 * 2 + i % 2)

    def on_y(value, d):
        return blk(value, lambda i: (i // 8 + d) % 4 * 8 + i % 8)

    def on_z(value, d):
        return lax.ppermute(value, "grp", [(i, (i + d) % groups) for i in range(groups)])

    sums = send_targets(block_list[0].T, block_counts, pair_targets[0], panels).reshape(panels, 24, ROWS * PANEL)
    targets = lax.all_to_all(sums, "blk", 0, 0, tiled=True)
    targets = targets.reshape(24 * panels, ROWS * PANEL)

    right = jnp.dot(emb, w_right, preferred_element_type=F32).astype(BF)
    ids = cluster_ids[0].astype(BF)
    ids_row = jnp.pad(ids[None, :], ((0, 15), (0, hidden - PANEL)))
    right_own = jnp.concatenate([right, ids_row], axis=0)
    right_outer = on_outer(right_own)
    right_partner = on_core(right_own)

    left = jnp.dot(emb, w_left, preferred_element_type=F32).astype(BF)
    outer_ids = right_outer[PANEL, :PANEL]
    partner_ids = right_partner[PANEL, :PANEL]
    before = jnp.where(me == 0, BF(-1), jnp.where(core == 0, outer_ids, partner_ids))
    after = jnp.where(me == panels - 1, BF(127), jnp.where(core == 0, partner_ids, outer_ids))
    col_ids = jnp.stack([before, ids, after])

    embs = [emb]
    for d in ORDER[1:]:
        embs.append(on_x(emb, d))

    lg, r_outer, r_own, keep, sent = pair_grads(
        core[None],
        col_ids.astype(jnp.int32),
        jnp.pad(col_ids.astype(F32), ((0, 5), (0, 0))),
        left,
        right_outer,
        right_own,
        right_partner,
        targets,
        hidden_bias[None, :],
        w_middle.T,
        w_final[:, None],
    )

    first = core == 0
    got = on_core(sent)
    over = lax.ppermute(r_outer, "blk", [(i, (i + 2) % panels) for i in range(1, panels, 2)]).astype(F32)
    outer = on_outer(r_outer).astype(F32)
    chip = []
    for piece in embs:
        chip += [piece, on_core(piece)]
    r_partner = sent[PANEL : 2 * PANEL].astype(F32)
    rg = (r_own.astype(F32) + got[PANEL : 2 * PANEL].astype(F32) + outer).astype(BF)
    pair_right = (got[:PANEL].astype(F32) + r_partner + over).astype(BF)
    extra = keep.astype(F32) + got[2 * PANEL :].astype(F32)
    both = jnp.concatenate(
        [jnp.where(first, lg, rg), jnp.where(first, got[:PANEL], pair_right), extra.astype(BF)], axis=0
    )
    grad_local = jnp.dot(lg, w_left.T, preferred_element_type=F32) + jnp.dot(
        rg, w_right.T, preferred_element_type=F32
    )

    def column(d):
        return lax.dynamic_slice_in_dim(both, ((x + d) & 3) * 128, 128, 1)

    parts = [column(0)]
    for d in ORDER[1:]:
        parts.append(on_x(column(d), d))
    total = weight_slice(chip, parts)
    piece = total.shape[0] // 4

    def rows(d):
        return lax.dynamic_slice_in_dim(total, ((y + d) & 3) * piece, piece, 0)

    parts = [rows(0)] + [on_y(rows(d), d) for d in ORDER[1:]]
    total = sum(p.astype(F32) for p in parts).astype(BF)
    total = (
        total.astype(F32)
        + lax.ppermute(total, "grp", [(i, i ^ 1) for i in range(groups)]).astype(F32)
    ).astype(BF)
    total = sum(p.astype(F32) for p in [total] + [on_z(total, d) for d in (2, 6, 4)]).astype(BF)
    total, grad_local = lax.optimization_barrier((total, grad_local))

    total = jnp.concatenate([total] + [on_y(total, d) for d in ORDER[1:]], axis=0)
    mine = [total] + [on_x(total, d) for d in ORDER[1:]]
    theirs = [on_core(p) for p in mine]
    devices = panels * groups
    scale = 1.0 / math.sqrt(devices * B_DEV * PANEL)
    vmem = pl.BlockSpec(memory_space=pltpu.VMEM)
    block = depth // 4
    grad_left, grad_right, grad_middle, grad_bias, grad_final = pl.pallas_call(
        lambda *refs: finish_kernel(scale, *refs),
        grid=(4,),
        out_shape=(
            jax.ShapeDtypeStruct((depth, hidden), F32),
            jax.ShapeDtypeStruct((depth, hidden), F32),
            jax.ShapeDtypeStruct((hidden, upper), F32),
            jax.ShapeDtypeStruct((1, hidden), F32),
            jax.ShapeDtypeStruct((1, upper), F32),
        ),
        in_specs=[pl.BlockSpec(memory_space=pltpu.SMEM)] + [vmem] * 8,
        out_specs=(
            pl.BlockSpec((block, hidden), lambda i: (i, 0)),
            pl.BlockSpec((block, hidden), lambda i: (i, 0)),
            pl.BlockSpec((hidden, upper), lambda i: (0, 0)),
            pl.BlockSpec((1, hidden), lambda i: (0, 0)),
            pl.BlockSpec((1, upper), lambda i: (0, 0)),
        ),
        scratch_shapes=[pltpu.VMEM((2, 4, 4 * piece, 128), BF)],
        compiler_params=pltpu.CompilerParams(vmem_limit_bytes=16 << 20),
        name="finish",
    )(jnp.stack([core, x, y]), *mine, *theirs)
    return (grad_local[None], grad_left, grad_right, grad_bias[0], grad_middle, grad_final[0])


def solution(mesh):
    return jax.shard_map(
        local,
        mesh=mesh,
        in_specs=(
            P("grp", "blk", None),
            P("grp", "blk"),
            P("grp", "blk", None),
            P("grp", "blk"),
            P("grp", "blk", None),
            P(),
            P(),
            P(),
            P(),
            P(),
        ),
        out_specs=(P("grp", "blk", None), P(), P(), P(), P(), P()),
        check_vma=False,
    )
```

```python
import math

import jax
import jax.numpy as jnp
from jax import lax
from jax.experimental import pallas as pl
from jax.experimental.pallas import tpu as pltpu
from jax.sharding import PartitionSpec as P

PANEL = 64
B_DEV = 8
ROWS = 8
CHUNK = 256
BF = jnp.bfloat16
F32 = jnp.float32


def forward(tile_at, left_s, right_s, hid_s, slope_s, rows=range(ROWS)):
    k = tile_at // 8
    left8 = left_s[pl.ds(pl.multiple_of(tile_at % 8 * ROWS, ROWS), ROWS), :]
    right = right_s[pl.ds(pl.multiple_of(k * PANEL, PANEL), PANEL), :]
    for a in rows:
        part = slice(a * PANEL, (a + 1) * PANEL)
        u = right.astype(BF) + jnp.broadcast_to(left8[a : a + 1, :], right.shape).astype(BF)
        p = jnp.tanh(u) + BF(1.0)
        h = u * p
        hid_s[part, :] = h
        slope_s[part, :] = p + h * (BF(2.0) - p)


def backward(
    tile_at, hid_s, slope_s, info_s, half_s, wmt_ref, wf_ref, lacc, racc, mid_acc, fin_acc
):
    col0 = pl.multiple_of(tile_at // 8 * PANEL, PANEL)
    row0 = pl.multiple_of(tile_at % 8 * ROWS, ROWS)
    wf = wf_ref[...]
    parts = [slice(c * CHUNK, (c + 1) * CHUNK) for c in range(ROWS * PANEL // CHUNK)]
    pre = [
        jnp.dot(hid_s[part, :], half_s[...], preferred_element_type=F32).T
        for part in parts
    ]
    terms, hiddens, fins = [], [], []
    for part, u in zip(parts, pre):
        p = jnp.tanh(u) + 1.0
        act = u * p
        predicted = jnp.sum(act * wf, axis=0, keepdims=True)
        pair_slope = info_s[tile_at, 1:2, part] * (
            info_s[tile_at, 2:3, part] * predicted - info_s[tile_at, 0:1, part]
        )
        grad_second = ((0.5 * pair_slope) * wf * (p + act * (2.0 - p))).astype(BF)
        fin = act * pair_slope
        fins.append(sum(fin[:, j * 128 : (j + 1) * 128] for j in range(CHUNK // 128)))
        hiddens.append(
            lax.dot_general(grad_second, wmt_ref[...], (((0,), (0,)), ((), ())), preferred_element_type=F32)
        )
        terms.append(jnp.dot(grad_second, hid_s[part, :], preferred_element_type=F32))
    fin_acc[...] += sum(fins)
    cols, rows = None, []
    for part, grad_hidden in zip(parts, hiddens):
        for a in range(CHUNK // PANEL):
            at = slice(part.start + a * PANEL, part.start + (a + 1) * PANEL)
            g = grad_hidden[a * PANEL : (a + 1) * PANEL, :] * slope_s[at, :].astype(F32)
            rows.append(jnp.sum(g, axis=0, keepdims=True))
            cols = g if cols is None else cols + g
    mid_acc[...] += sum(terms)
    racc[pl.ds(col0, PANEL), :] += cols
    lacc[pl.ds(row0, ROWS), :] += jnp.concatenate(rows, axis=0)


def pair_kernel(
    core,
    ids_s,
    ids_ref,
    left_ref,
    right_o,
    right_m,
    right_p,
    targets_ref,
    bias_ref,
    wmt_ref,
    wf_ref,
    out_left,
    out_outer,
    out_own,
    out_keep,
    out_sent,
    todo,
    panels_s,
    sems,
    left_s,
    right_s,
    info_s,
    half_s,
    hid_s,
    slope_s,
    lacc,
    racc,
    mid_acc,
    fin_acc,
):
    hidden = left_ref.shape[1]
    tile = ROWS * PANEL
    loads = [
        pltpu.make_async_copy(ref.at[0:PANEL, :], panels_s.at[n], sems.at[m])
        for m, (n, ref) in enumerate(
            ((0, left_ref), (1 + 2 * core[0], right_o), (2, right_m), (3 - 2 * core[0], right_p))
        )
    ]
    for copy in loads:
        copy.start()
    iota = lambda shape, axis: lax.broadcasted_iota(jnp.int32, shape, axis)
    begin = jnp.sum(jnp.where((ids_ref[...] < ids_s[1, PANEL // 2].astype(F32)) & (iota((8, PANEL), 0) < 3), 1, 0))
    shift = PANEL - (begin & (PANEL - 1))

    def scan(i, n):
        j, rt = i // 8, i % 8
        start = jnp.maximum(j * PANEL - shift, 0)
        end = jnp.minimum(j * PANEL - shift + PANEL - 1, 3 * PANEL - 1)
        last = jnp.maximum(end, 0)
        meets = (
            (end >= 0)
            & (ids_s[1, rt * ROWS] <= ids_s[last // PANEL, last % PANEL])
            & (ids_s[start // PANEL, start % PANEL] <= ids_s[1, rt * ROWS + ROWS - 1])
        )
        todo[n] = i
        return n + meets.astype(jnp.int32)

    n_todo = lax.fori_loop(0, 32, scan, 0)
    half_s[...] = (wmt_ref[...].astype(F32) * 0.5).T.astype(BF)
    n_src = targets_ref.shape[0]
    tsum = jnp.dot(
        (iota((24, n_src), 1) % 24 == iota((24, n_src), 0)).astype(BF), targets_ref[...], preferred_element_type=F32
    )
    ids = ids_ref[...]
    spread = (iota((PANEL, tile), 0) % ROWS == iota((PANEL, tile), 1) // PANEL).astype(BF)
    repeat = (iota((PANEL, tile), 0) == iota((PANEL, tile), 1) % PANEL).astype(BF)
    row_ids = jnp.where(iota((8, PANEL), 1) // ROWS == iota((8, PANEL), 0), ids[1:2, :], 0.0)
    row_ids = jnp.dot(row_ids.astype(BF), spread, preferred_element_type=F32)
    col_ids = jnp.dot(ids.astype(BF), repeat, preferred_element_type=F32)
    lane = iota((8, tile), 1)
    itself = iota((8, tile), 0) * ROWS + lane // PANEL == lane % PANEL
    infos = []
    for k in range(3):
        same = row_ids == col_ids[k : k + 1, :]
        mask = jnp.where(same & ~itself if k == 1 else same, 16.0, 0.0)
        count = jnp.max(
            jnp.where(iota((1, tile), 1) == k * (PANEL + 1), tsum[8:9, :], 0.0), axis=1, keepdims=True
        )
        infos.append((tsum[k * 8 : k * 8 + 8, :], mask, jnp.broadcast_to(count, (8, tile))))
    ahead, behind = lax.rem(shift, tile), lax.rem(shift + tile - PANEL, tile)
    for j in range(4):
        for n in range(3):
            here = pltpu.roll(infos[j][n], ahead, 1) if j < 3 else jnp.zeros((8, tile), F32)
            before = pltpu.roll(infos[j - 1][n], behind, 1) if j > 0 else jnp.zeros((8, tile), F32)
            moved = jnp.where(lane % PANEL >= shift, here, before)
            for rt in range(8):
                info_s[j * 8 + rt, n : n + 1, :] = moved[rt : rt + 1, :]
    lacc[...] = jnp.zeros_like(lacc)
    racc[...] = jnp.zeros_like(racc)
    mid_acc[...] = jnp.zeros_like(mid_acc)
    fin_acc[...] = jnp.zeros_like(fin_acc)
    for copy in loads:
        copy.wait()
    left_s[...] = (panels_s[0].astype(F32) + bias_ref[...]) * 0.5
    place = (iota((4 * PANEL, 3 * PANEL), 0) == iota((4 * PANEL, 3 * PANEL), 1) + shift).astype(BF)
    rights = jnp.concatenate([panels_s[k + 1] for k in range(3)], axis=0)
    right_s[...] = jnp.dot(place, rights, preferred_element_type=F32) * 0.5
    rest = (info_s, half_s, wmt_ref, wf_ref, lacc, racc, mid_acc, fin_acc)

    def step(i, carry):
        forward(todo[i], left_s, right_s, hid_s, slope_s)
        backward(todo[i], hid_s, slope_s, *rest)
        return carry

    lax.fori_loop(0, n_todo, step, 0)
    left = lacc[...] * 0.5
    out_left[...] = left.astype(BF)
    back = (iota((3 * PANEL, 4 * PANEL), 1) == iota((3 * PANEL, 4 * PANEL), 0) + shift).astype(BF)
    total = racc[...] * 0.5
    high = total.astype(BF)
    low = (total - high.astype(F32)).astype(BF)
    right_s[0 : 3 * PANEL, :] = jnp.dot(back, high, preferred_element_type=F32) + jnp.dot(
        back, low, preferred_element_type=F32
    )
    at = pl.multiple_of(2 * PANEL * core[0], PANEL)
    outer = right_s[pl.ds(at, PANEL), :].astype(BF)
    own = right_s[PANEL : 2 * PANEL, :].astype(BF)
    partner = right_s[pl.ds(pl.multiple_of(2 * PANEL - at, PANEL), PANEL), :].astype(BF)
    out_outer[...] = outer
    out_own[...] = own
    out_sent[PANEL : 2 * PANEL, :] = partner

    def middle(ref, start):
        for j in range(hidden // 128):
            block = slice(j * 128, (j + 1) * 128)
            ref[start : start + 128, block] = mid_acc[:, block].T.astype(BF)

    def small(ref, start):
        ref[start : start + 128, :] = jnp.zeros((128, hidden), BF)
        ref[start : start + 1, :] = jnp.sum(left, axis=0, keepdims=True).astype(BF)
        ref[start + 16 : start + 17, 0:128] = jnp.sum(fin_acc[...].T, axis=0, keepdims=True).astype(BF)

    @pl.when(core[0] == 0)
    def _():
        out_sent[0:PANEL, :] = own
        small(out_sent, 2 * PANEL)
        middle(out_keep, 0)

    @pl.when(core[0] != 0)
    def _():
        out_sent[0:PANEL, :] = left.astype(BF)
        middle(out_sent, 2 * PANEL)
        small(out_keep, 0)


def pair_grads(core, ids_s, ids, left, right_o, right_m, right_p, targets, bias, wmt, wf):
    hidden = left.shape[1]
    upper = wmt.shape[0]
    tile = ROWS * PANEL
    vmem = pl.BlockSpec(memory_space=pltpu.VMEM)
    panel = jax.ShapeDtypeStruct((PANEL, hidden), BF)
    return pl.pallas_call(
        pair_kernel,
        out_shape=(
            panel,
            panel,
            panel,
            jax.ShapeDtypeStruct((upper, hidden), BF),
            jax.ShapeDtypeStruct((2 * PANEL + upper, hidden), BF),
        ),
        in_specs=[pl.BlockSpec(memory_space=pltpu.SMEM)] * 2
        + [vmem]
        + [pl.BlockSpec(memory_space=pltpu.HBM)] * 4
        + [vmem] * 4,
        out_specs=(vmem,) * 5,
        scratch_shapes=[
            pltpu.SMEM((40,), jnp.int32),
            pltpu.VMEM((4, PANEL, hidden), BF),
            pltpu.SemaphoreType.DMA((4,)),
            pltpu.VMEM((PANEL, hidden), F32),
            pltpu.VMEM((4 * PANEL, hidden), F32),
            pltpu.VMEM((32, 8, tile), F32),
            pltpu.VMEM((hidden, upper), BF),
            pltpu.VMEM((tile, hidden), BF),
            pltpu.VMEM((tile, hidden), BF),
            pltpu.VMEM((PANEL, hidden), F32),
            pltpu.VMEM((4 * PANEL, hidden), F32),
            pltpu.VMEM((upper, hidden), F32),
            pltpu.VMEM((upper, 128), F32),
        ],
        compiler_params=pltpu.CompilerParams(vmem_limit_bytes=24 << 20),
        cost_estimate=pl.CostEstimate(
            flops=10 * 24 * tile * hidden * upper, bytes_accessed=2 << 20, transcendentals=24 * tile * hidden
        ),
        name="pair_grads",
    )(core, ids_s, ids, *[pltpu.with_memory_space_constraint(v, pltpu.HBM) for v in (left, right_o, right_m, right_p)], targets, bias, wmt, wf)


def send_kernel(blocks, live, targets_hbm, out_ref, acc, targets_ref, sem):
    tile = out_ref.shape[1]
    load = pltpu.make_async_copy(targets_hbm, targets_ref, sem)
    load.start()
    acc[...] = jnp.zeros_like(acc)
    load.wait()
    lane = lax.broadcasted_iota(jnp.int32, (1, tile), 1)
    counters = (lane == 0) | (lane == PANEL + 1) | (lane == 2 * (PANEL + 1))

    def slot(i, carry):
        row = blocks[0, i]
        side = blocks[1, i] - row + 1
        to = row * 3 + side
        for rt in range(8):
            value = targets_ref[pl.ds(i, 1), rt * tile : (rt + 1) * tile]
            if rt == 0:
                value = jnp.where(counters & (side == 1), 0.0, value)
            acc[to, rt : rt + 1, :] += value
        acc[row * 3 + 1, 0:1, :] += jnp.where(lane == side * (PANEL + 1), 1.0, 0.0)
        return carry

    lax.fori_loop(0, live[0, 0], slot, 0)
    for p in range(acc.shape[0]):
        out_ref[p * 8 : (p + 1) * 8, :] = acc[p].astype(BF)


def send_targets(blocks, live, targets, panels):
    tile = ROWS * PANEL
    smem = pl.BlockSpec(memory_space=pltpu.SMEM)
    vmem = pl.BlockSpec(memory_space=pltpu.VMEM)
    return pl.pallas_call(
        send_kernel,
        out_shape=jax.ShapeDtypeStruct((24 * panels, tile), BF),
        in_specs=[smem, smem, pl.BlockSpec(memory_space=pltpu.HBM)],
        out_specs=vmem,
        scratch_shapes=[
            pltpu.VMEM((3 * panels, 8, tile), F32),
            pltpu.VMEM(targets.shape, F32),
            pltpu.SemaphoreType.DMA(()),
        ],
        compiler_params=pltpu.CompilerParams(vmem_limit_bytes=8 << 20),
        name="send_targets",
    )(blocks, live, pltpu.with_memory_space_constraint(targets, pltpu.HBM))


def slice_kernel(*refs):
    embs, parts, out, emb_s, part_s = refs[:8], refs[8:12], refs[12], refs[13], refs[14]
    rows, depth = embs[0].shape
    for n, ref in enumerate(embs):
        emb_s[n * rows : (n + 1) * rows, :] = ref[...]
    for n, ref in enumerate(parts):
        part_s[n * 2 * rows : (n + 1) * 2 * rows, :] = ref[0 : 2 * rows, :]
    out[0:depth, :] = lax.dot_general(
        emb_s[...], part_s[...], (((0,), (0,)), ((), ())), preferred_element_type=F32
    ).astype(BF)
    out[depth:, :] = sum(ref[2 * rows :, :].astype(F32) for ref in parts).astype(BF)


def weight_slice(embs, parts):
    rows, depth = embs[0].shape
    width = parts[0].shape[1]
    vmem = pl.BlockSpec(memory_space=pltpu.VMEM)
    return pl.pallas_call(
        slice_kernel,
        out_shape=jax.ShapeDtypeStruct((depth + parts[0].shape[0] - 2 * rows, width), BF),
        in_specs=[vmem] * 12,
        out_specs=vmem,
        scratch_shapes=[pltpu.VMEM((8 * rows, depth), BF), pltpu.VMEM((8 * rows, width), BF)],
        compiler_params=pltpu.CompilerParams(vmem_limit_bytes=16 << 20),
        name="weight_slice",
    )(*embs, *parts)


ORDER = (0, 1, 3, 2)


def finish_kernel(scale, pos, *refs):
    pieces, (left_ref, right_ref, mid_ref, bias_ref, fin_ref, whole) = refs[:8], refs[8:]
    part = whole.shape[2] // 4
    depth = whole.shape[2] - 128
    block = left_ref.shape[0]

    @pl.when(pl.program_id(0) == 0)
    def _():
        for n, ref in enumerate(pieces):
            side = pos[0] if n < 4 else 1 - pos[0]
            column = lax.rem(pos[1] - ORDER[n % 4] + 4, 4)
            for m, dy in enumerate(ORDER):
                row = pl.multiple_of(lax.rem(pos[2] - dy + 4, 4) * part, 32)
                whole[side, column, pl.ds(row, part), :] = ref[m * part : (m + 1) * part, :]
        for j in range(4):
            lanes = slice(j * 128, (j + 1) * 128)
            mid_ref[lanes, :] = whole[0, j, depth : depth + 128, :].astype(F32) * scale
            bias_ref[:, lanes] = whole[1, j, depth : depth + 1, :].astype(F32) * scale
        fin_ref[...] = whole[1, 0, depth + 16 : depth + 17, :].astype(F32) * scale

    rows = pl.ds(pl.multiple_of(pl.program_id(0) * block, block), block)
    for j in range(4):
        lanes = slice(j * 128, (j + 1) * 128)
        left_ref[:, lanes] = whole[0, j, rows, :].astype(F32) * scale
        right_ref[:, lanes] = whole[1, j, rows, :].astype(F32) * scale


def local(
    embeddings,
    cluster_ids,
    block_list,
    block_counts,
    pair_targets,
    w_left,
    w_right,
    hidden_bias,
    w_middle,
    w_final,
):
    emb = embeddings[0]
    depth = emb.shape[1]
    hidden = w_left.shape[1]
    upper = w_middle.shape[1]
    panels = lax.axis_size("blk")
    groups = lax.axis_size("grp")
    me = lax.axis_index("blk")
    core, x, y = me & 1, (me >> 1) & 3, me >> 3

    def blk(value, partner):
        return lax.ppermute(value, "blk", [(i, partner(i)) for i in range(panels)])

    def on_core(value):
        return blk(value, lambda i: i ^ 1)

    def on_outer(value):
        return blk(value, lambda i: (i - 1 if i % 2 == 0 else i + 1) % panels)

    def on_x(value, d):
        return blk(value, lambda i: i // 8 * 8 + (i // 2 % 4 + d) % 4 * 2 + i % 2)

    def on_y(value, d):
        return blk(value, lambda i: (i // 8 + d) % 4 * 8 + i % 8)

    def on_z(value, d):
        return lax.ppermute(value, "grp", [(i, (i + d) % groups) for i in range(groups)])

    sums = send_targets(block_list[0].T, block_counts, pair_targets[0], panels).reshape(panels, 24, ROWS * PANEL)
    targets = lax.all_to_all(sums, "blk", 0, 0, tiled=True)
    targets = targets.reshape(24 * panels, ROWS * PANEL)

    right = jnp.dot(emb, w_right, preferred_element_type=F32).astype(BF)
    ids = cluster_ids[0].astype(BF)
    ids_row = jnp.pad(ids[None, :], ((0, 15), (0, hidden - PANEL)))
    right_own = jnp.concatenate([right, ids_row], axis=0)
    right_outer = on_outer(right_own)
    right_partner = on_core(right_own)

    left = jnp.dot(emb, w_left, preferred_element_type=F32).astype(BF)
    outer_ids = right_outer[PANEL, :PANEL]
    partner_ids = right_partner[PANEL, :PANEL]
    before = jnp.where(me == 0, BF(-1), jnp.where(core == 0, outer_ids, partner_ids))
    after = jnp.where(me == panels - 1, BF(127), jnp.where(core == 0, partner_ids, outer_ids))
    col_ids = jnp.stack([before, ids, after])

    embs = [emb]
    for d in ORDER[1:]:
        embs.append(on_x(emb, d))

    lg, r_outer, r_own, keep, sent = pair_grads(
        core[None],
        col_ids.astype(jnp.int32),
        jnp.pad(col_ids.astype(F32), ((0, 5), (0, 0))),
        left,
        right_outer,
        right_own,
        right_partner,
        targets,
        hidden_bias[None, :],
        w_middle.T,
        w_final[:, None],
    )

    first = core == 0
    got = on_core(sent)
    over = lax.ppermute(r_outer, "blk", [(i, (i + 2) % panels) for i in range(1, panels, 2)]).astype(F32)
    outer = on_outer(r_outer).astype(F32)
    chip = []
    for piece in embs:
        chip += [piece, on_core(piece)]
    r_partner = sent[PANEL : 2 * PANEL].astype(F32)
    rg = (r_own.astype(F32) + got[PANEL : 2 * PANEL].astype(F32) + outer).astype(BF)
    pair_right = (got[:PANEL].astype(F32) + r_partner + over).astype(BF)
    extra = keep.astype(F32) + got[2 * PANEL :].astype(F32)
    both = jnp.concatenate(
        [jnp.where(first, lg, rg), jnp.where(first, got[:PANEL], pair_right), extra.astype(BF)], axis=0
    )
    grad_local = jnp.dot(lg, w_left.T, preferred_element_type=F32) + jnp.dot(
        rg, w_right.T, preferred_element_type=F32
    )

    def column(d):
        return lax.dynamic_slice_in_dim(both, ((x + d) & 3) * 128, 128, 1)

    parts = [column(0)]
    for d in ORDER[1:]:
        parts.append(on_x(column(d), d))
    total = weight_slice(chip, parts)
    piece = total.shape[0] // 4

    def rows(d):
        return lax.dynamic_slice_in_dim(total, ((y + d) & 3) * piece, piece, 0)

    parts = [rows(0)] + [on_y(rows(d), d) for d in ORDER[1:]]
    total = sum(p.astype(F32) for p in parts).astype(BF)
    total = (
        total.astype(F32)
        + lax.ppermute(total, "grp", [(i, i ^ 1) for i in range(groups)]).astype(F32)
    ).astype(BF)
    total = sum(p.astype(F32) for p in [total] + [on_z(total, d) for d in (2, 6, 4)]).astype(BF)
    total, grad_local = lax.optimization_barrier((total, grad_local))

    total = jnp.concatenate([total] + [on_y(total, d) for d in ORDER[1:]], axis=0)
    mine = [total] + [on_x(total, d) for d in ORDER[1:]]
    theirs = [on_core(p) for p in mine]
    devices = panels * groups
    scale = 1.0 / math.sqrt(devices * B_DEV * PANEL)
    vmem = pl.BlockSpec(memory_space=pltpu.VMEM)
    block = depth // 4
    grad_left, grad_right, grad_middle, grad_bias, grad_final = pl.pallas_call(
        lambda *refs: finish_kernel(scale, *refs),
        grid=(4,),
        out_shape=(
            jax.ShapeDtypeStruct((depth, hidden), F32),
            jax.ShapeDtypeStruct((depth, hidden), F32),
            jax.ShapeDtypeStruct((hidden, upper), F32),
            jax.ShapeDtypeStruct((1, hidden), F32),
            jax.ShapeDtypeStruct((1, upper), F32),
        ),
        in_specs=[pl.BlockSpec(memory_space=pltpu.SMEM)] + [vmem] * 8,
        out_specs=(
            pl.BlockSpec((block, hidden), lambda i: (i, 0)),
            pl.BlockSpec((block, hidden), lambda i: (i, 0)),
            pl.BlockSpec((hidden, upper), lambda i: (0, 0)),
            pl.BlockSpec((1, hidden), lambda i: (0, 0)),
            pl.BlockSpec((1, upper), lambda i: (0, 0)),
        ),
        scratch_shapes=[pltpu.VMEM((2, 4, 4 * piece, 128), BF)],
        compiler_params=pltpu.CompilerParams(vmem_limit_bytes=16 << 20),
        name="finish",
    )(jnp.stack([core, x, y]), *mine, *theirs)
    return (grad_local[None], grad_left, grad_right, grad_bias[0], grad_middle, grad_final[0])


def solution(mesh):
    return jax.shard_map(
        local,
        mesh=mesh,
        in_specs=(
            P("grp", "blk", None),
            P("grp", "blk"),
            P("grp", "blk", None),
            P("grp", "blk"),
            P("grp", "blk", None),
            P(),
            P(),
            P(),
            P(),
            P(),
        ),
        out_specs=(P("grp", "blk", None), P(), P(), P(), P(), P()),
        check_vma=False,
    )
```
